32 devices in a mesh: grp: 2 (over y), brick: 16 (over z, x, core).
Axes of the slice: x: 2, y: 2, z: 4, core: 2. Of those that a mesh axis runs over, the one named last changes fastest.
Arguments:
- low_factor: float32 [64, 16, 32, 512], P('brick', None, None, 'grp'), may hold values from -70 to 70, as said below
- test_matrix: float32 [512, 256], P('grp'), may hold values from -0.25 to 0.25
Outputs:
- basis: float32 [64, 16, 32, 256], P('brick')
- projected: float32 [256, 512], P(None, 'grp')
The draws below stay inside these ranges and needn't reach their ends.
Inputs may be any that keep to these rules, and one draw needn't show every extreme that they name: `low_factor`: A dense real factor.
All inputs are finite; a program needn't handle non-finite values.
Results may differ from the reference program's by a relative error of at most 0.0003.
Values sent between devices are 32-bit elements; how exact they have to be, the bound alone decides.
A program may use at most 64 MiB of HBM per device.

```python
import jax
import jax.numpy as jnp
from jax import lax

NY = 16
NZ = 32
GCOL = 256
RANK = 256
K = 512
NX = 64
N_GRP = 2


def draw_low_factor(key, part):
    keys = jax.random.split(jax.random.fold_in(key, 11), 3)
    shape = (NX, NY, NZ, K)
    values = jnp.clip(jax.random.normal(keys[0], shape, jnp.float32), -6.0, 6.0)
    position = jnp.arange(NX, dtype=jnp.float32) / jnp.float32(max(NX - 1, 1))
    rising = jnp.exp(jnp.log(3.0) * position)[:, None, None, None]
    cell_scale = jnp.exp(jax.random.uniform(keys[1], (NX, NY, NZ, 1), jnp.float32) * jnp.log(3.4))
    column_scale = jnp.exp(jax.random.uniform(keys[2], (1, 1, 1, K), jnp.float32) * jnp.log(10.0))
    scaled = values * rising * cell_scale * column_scale / 3.0
    return jnp.clip(scaled, -70.0, 70.0).astype(jnp.float32)


def block_levels(stream_key, shape, cuts, low, top_value):
    def one(dim, shards_of):
        steps = jax.random.uniform(jax.random.fold_in(jax.random.fold_in(stream_key, 6), dim), (shards_of,), jnp.float32, low / len(cuts), top_value / len(cuts))
        return jnp.repeat(jnp.exp(steps), shape[dim] // shards_of).reshape((-1,) + (1,) * (len(shape) - dim - 1))

    gain = one(*cuts[0])
    for cut in cuts[1:]:
        gain = gain * one(*cut)
    return gain


def normal_values(key, extent, width, limit, shards=(), held_as=jnp.bfloat16):
    values = jax.random.normal(key, extent, jnp.float32) * width
    if len(shards) > 0:
        values = block_levels(key, extent, shards, -0.22, 0.18) * values
    return jnp.clip(values, min=-limit, max=limit).astype(held_as)


def setup_inputs(seed: int = 0) -> dict:
    key_list = jax.random.split(jax.random.key(seed), 3)
    return {
        "low_factor": draw_low_factor(jax.random.fold_in(key_list[2], 71), 0),
        "test_matrix": normal_values(key_list[1], (K, RANK), K ** -0.5, 0.25, ((0, 2),), jnp.float32),
    }


DIFF = 0.12
CONV = 0.08
HIGH = lax.Precision.HIGHEST

def operate(field):
    padded = jnp.pad(field, ((1, 1), (1, 1), (1, 1), (0, 0)))
    xminus = padded[:-2, 1:-1, 1:-1]
    xplus = padded[2:, 1:-1, 1:-1]
    beside_all = xminus + xplus + padded[1:-1, :-2, 1:-1] + padded[1:-1, 2:, 1:-1]
    beside_all = beside_all + padded[1:-1, 1:-1, :-2] + padded[1:-1, 1:-1, 2:]
    return field - DIFF * beside_all - CONV * (xminus - xplus)

def reference(low_factor, test_matrix):
    cells = NX * NY * NZ

    def grown_group(group):
        start = (group * GCOL).astype(jnp.int32)
        piece = lax.dynamic_slice_in_dim(low_factor, start, GCOL, 3)
        return operate(operate(piece)).reshape(cells, GCOL)

    def add_group(group, total):
        start = (group * GCOL).astype(jnp.int32)
        omega = lax.dynamic_slice_in_dim(test_matrix, start, GCOL, 0)
        return total + jnp.dot(grown_group(group).astype(jnp.float32), omega.astype(jnp.float32), precision=HIGH, preferred_element_type=jnp.float32)
    sketch = lax.fori_loop(jnp.int32(0), jnp.int32(N_GRP), add_group, jnp.zeros((cells, RANK), jnp.float32))
    gram = lax.dot_general(sketch, sketch, (((0,), (0,)), ((), ())), precision=HIGH)
    lower = jnp.linalg.cholesky(gram)
    orthonormal = lax.linalg.triangular_solve(lower, sketch, left_side=False, lower=True, transpose_a=True)

    def project_group(group):
        return lax.dot_general(orthonormal, grown_group(group), (((0,), (0,)), ((), ())), precision=HIGH)
    blocks = lax.map(project_group, jnp.arange(N_GRP, dtype=jnp.int32))
    projected = jnp.moveaxis(blocks, 0, 1).reshape(RANK, K)
    basis = (orthonormal * jnp.sqrt(jnp.float32(cells))).reshape(NX, NY, NZ, RANK)
    return (basis, projected)
```

```python
import functools

import jax
import jax.numpy as jnp
from jax import lax
from jax.experimental import pallas as pl
from jax.experimental.pallas import tpu as pltpu
from jax.sharding import PartitionSpec as P

DIFF = 0.12
CONV = 0.08
HIGH = lax.Precision.HIGHEST
MESH = pl.DeviceIdType.MESH
BLOCK = 32
GROUP = 8
LANES = 128
LEAD = 3
AHEAD = 2
WINDOW = 4
FIRST_BACK = 3
SECOND_BACK = 6
HOOK_SCATTER = 5
HOOK_CROSS = 7
PIECES = 4


def dot(left, right, dims):
    return lax.dot_general(
        left, right, (dims, ((), ())), precision=HIGH, preferred_element_type=jnp.float32
    )


def split(value):
    high = value.astype(jnp.bfloat16)
    return high, (value - high.astype(jnp.float32)).astype(jnp.bfloat16)


def pass_dot(left, right, dims):
    return lax.dot_general(left, right, (dims, ((), ())), preferred_element_type=jnp.float32)


def parts_dot(left, right, dims):
    return (
        pass_dot(left[0], right[0], dims)
        + pass_dot(left[0], right[1], dims)
        + pass_dot(left[1], right[0], dims)
    )


def share(rows, chips):
    return max(k for k in range(1, chips + 1) if rows % (8 * k) == 0)


def batches(groups, seg, span_y):
    if groups != 2 or seg < 4 or seg % 2:
        return [(span_y - 1, [p]) for p in range(seg)]
    mid = seg // 2
    plan = [(seg + mid + t, [mid + t, mid - 1 - t]) for t in range(mid - 1)]
    return plan + [(span_y - 1, [seg - 1]), (span_y - 1, [0])]


def packed_rows(rank):
    blocks = rank // LANES
    return LANES * blocks * (blocks + 1) // 2


def tiles(rank):
    blocks = rank // LANES
    return [(i, j) for i in range(blocks) for j in range(i, blocks)]


def kernel(
    dims, x_hbm, omega_hbm, sketch_out, inverse_out, proj_out,
    omega, omega_high, omega_low, ext, first, grown, cross, sketch, gram, gram_mixed, packed, gram_rx, gram_strips,
    gram_y, gram_full, proj, proj_rx, proj_strips, proj_strip, proj_y, proj_full, both,
    local_sem, out_sem, halo_send, halo_recv, row_send, row_recv, back_send, back_recv,
    spread_sem, omega_sem, gram_sem, proj_sem,
):
    groups, bricks, slab, span_y, span_z, cells = dims
    cols, rank = omega.shape[1:]
    chips = bricks // 2
    seg = span_y // groups
    me_g = lax.axis_index("grp")
    me_b = lax.axis_index("brick")
    chip, core = me_b // 2, lax.rem(me_b, 2)
    upward = me_g >= groups // 2
    chunks = span_y - LEAD + 1
    half_packed = packed_rows(rank) // 2
    gram_owners = share(half_packed, chips)
    gram_strip = half_packed // gram_owners
    proj_owners = share(rank // 2, chips)
    proj_strip_rows = rank // 2 // proj_owners
    omega_owners = share(cols // 2, chips)
    omega_strip = cols // 2 // omega_owners
    plan = batches(groups, seg, span_y)
    order = [p for _, rows in plan for p in rows]

    def device(g, b):
        return {"grp": g, "brick": b}

    def other_group(d):
        return lax.rem(me_g + d, groups)

    def chip_peer(d):
        return lax.rem(chip + d, chips)

    sibling = device(me_g, me_b + 1 - 2 * core)
    barrier = pltpu.get_barrier_semaphore()

    def greet(g, b):
        pl.semaphore_signal(barrier, inc=1, device_id=device(g, b), device_id_type=MESH)

    def remote(source, sink, send, recv, to):
        return pltpu.make_async_remote_copy(
            src_ref=source, dst_ref=sink, send_sem=send, recv_sem=recv,
            device_id=to, device_id_type=MESH,
        )

    def bytes_wait(ref, sem):
        pltpu.make_async_copy(ref, ref, sem).wait()

    outer = jnp.where(core == 0, me_b - 1, me_b + 1)
    has_outer = jnp.logical_and(outer >= 0, outer < bricks)
    with jax.named_scope("greet"):
        for d in range(1, groups):
            greet(other_group(d), me_b)
        lax.fori_loop(1, chips, lambda d, c: (greet(me_g, chip_peer(d) * 2 + core), c)[1], 0)

        @pl.when(has_outer)
        def _():
            greet(me_g, outer)

        greet(me_g, me_b + 1 - 2 * core)

    mine = pltpu.make_async_copy(
        x_hbm, ext.at[pl.ds(2, slab), pl.ds(1, span_y)], local_sem.at[0]
    )
    mine.start()
    weights = pltpu.make_async_copy(omega_hbm, omega.at[me_g], local_sem.at[1])
    weights.start()
    layer = (span_z, cols)
    for y in (0, span_y + 1):
        ext[:, y] = jnp.zeros((slab + 4,) + layer, jnp.float32)
        first[:, y] = jnp.zeros((slab + 2,) + layer, jnp.float32)

    @pl.when(me_b == 0)
    def _():
        ext[0:2] = jnp.zeros((2, span_y + 2) + layer, jnp.float32)

    @pl.when(me_b == bricks - 1)
    def _():
        ext[slab + 2 :] = jnp.zeros((2, span_y + 2) + layer, jnp.float32)

    with jax.named_scope("barrier"):
        pl.semaphore_wait(barrier, groups - 1 + chips + jnp.where(has_outer, 1, 0))

    def row_at(i, count=1):
        return jnp.where(upward, i, span_y - i - count)

    def halo(k, up):
        if isinstance(k, int) and k == 0:
            start, rows = row_at(0, LEAD), LEAD
        else:
            start, rows = row_at(k + LEAD - 1), 1
        side = 0 if up else 1
        return remote(
            x_hbm.at[pl.ds(slab - 2 if up else 0, 2), pl.ds(start, rows)],
            ext.at[pl.ds(0 if up else slab + 2, 2), pl.ds(1 + start, rows)],
            halo_send.at[side, k], halo_recv.at[side, k],
            device(me_g, me_b + 1 if up else me_b - 1),
        )

    def halo_start(k):
        @pl.when(me_b < bricks - 1)
        def _():
            halo(k, True).start()

        @pl.when(me_b > 0)
        def _():
            halo(k, False).start()

    def halo_wait(k):
        @pl.when(me_b > 0)
        def _():
            halo(k, True).wait_recv()

        @pl.when(me_b < bricks - 1)
        def _():
            halo(k, False).wait_recv()

    for k in range(AHEAD):
        halo_start(k)
    weights.wait()

    def omega_at(g, o, c):
        return omega.at[g, pl.ds(pl.multiple_of((c * omega_owners + o) * omega_strip, 8), omega_strip)]

    def spread(d):
        here = omega_at(me_g, chip, core)
        return remote(here, here, spread_sem.at[0, d - 1], spread_sem.at[1, d - 1], device(other_group(d), me_b))

    def guarded(owners, index, action):
        if owners == chips:
            action()
        else:
            pl.when(index < owners)(action)

    def spread_start():
        for d in range(1, groups):
            spread(d).start()

    guarded(omega_owners, chip, spread_start)
    mine.wait()

    def operate(mid, low, high, before, after):
        z = lax.broadcasted_iota(jnp.int32, mid.shape, mid.ndim - 2)
        down = jnp.where(z == 0, 0.0, pltpu.roll(mid, 1, mid.ndim - 2))
        up = jnp.where(z == span_z - 1, 0.0, pltpu.roll(mid, span_z - 1, mid.ndim - 2))
        beside = low + high + before + after + down + up
        return mid - DIFF * beside - CONV * (low - high)

    gate_low = jnp.where(me_b == 0, 0.0, 1.0)
    gate_high = jnp.where(me_b == bricks - 1, 0.0, 1.0)

    def first_row(i):
        y = row_at(i)
        for i in range(slab + 2):
            value = operate(
                ext[i + 1, y + 1], ext[i, y + 1], ext[i + 2, y + 1], ext[i + 1, y], ext[i + 1, y + 2]
            )
            if i == 0:
                value = value * gate_low
            if i == slab + 1:
                value = value * gate_high
            first[i, y + 1] = value

    def second_row(i):
        y = row_at(i)
        for i in range(slab):
            grown[y, i] = operate(
                first[i + 1, y + 1], first[i, y + 1], first[i + 2, y + 1],
                first[i + 1, y], first[i + 1, y + 2],
            )

    def row_copy(y, owner):
        d = lax.rem(owner - me_g + groups, groups)
        at = y - owner * seg
        return remote(
            grown.at[y], cross.at[d - 1, at],
            row_send.at[y], row_recv.at[d - 1, at], device(owner, me_b),
        )

    def step(i):
        with jax.named_scope("row"):
            second_row(i)
        y = row_at(i)
        owner = y // seg

        @pl.when(owner != me_g)
        def _():
            row_copy(y, owner).start()

    with jax.named_scope("halo0"):
        halo_wait(0)
    first_row(0)
    first_row(1)
    for k in range(AHEAD, min(WINDOW + 1, chunks)):
        halo_start(k)
    step(0)

    def body(i, carry):
        halo_wait(i)
        first_row(i + 1)
        step(i)

        @pl.when(i + WINDOW < chunks)
        def _():
            halo_start(i + WINDOW)

        return carry

    def gather_start(buf, at, sem, owners):
        def send():
            def one(d, carry):
                here = at(buf, chip)
                remote(here, here, sem.at[0], sem.at[1], device(me_g, chip_peer(d) * 2 + core)).start()
                return carry

            lax.fori_loop(1, chips, one, 0)

        guarded(owners, chip, send)

    def gather_finish(received, all_but_one, sent, sem, owners):
        if owners == chips:
            bytes_wait(all_but_one, sem.at[1])
            bytes_wait(all_but_one, sem.at[0])
        else:
            @pl.when(chip < owners)
            def _():
                bytes_wait(all_but_one, sem.at[1])
                bytes_wait(sent, sem.at[0])

            @pl.when(chip >= owners)
            def _():
                bytes_wait(received, sem.at[1])

    middle = max(span_y // 4, 1)
    lax.fori_loop(1, middle, body, 0)

    def omega_half(g, c, strips):
        return omega.at[g, pl.ds(pl.multiple_of(c * (cols // 2), 8), strips * omega_strip)]

    def omega_gather(d):
        g = lax.rem(me_g - d + groups, groups)
        guarded(omega_owners, chip, lambda: spread(d).wait_recv())
        gather_start(omega.at[g], lambda ref, o: ref.at[
            pl.ds(pl.multiple_of((core * omega_owners + o) * omega_strip, 8), omega_strip)
        ], omega_sem.at[d - 1, 0], omega_owners)

    with jax.named_scope("omega_a"):
        for d in range(1, groups):
            omega_gather(d)
    lax.fori_loop(middle, 2 * middle, body, 0)

    def omega_pair(d):
        g = lax.rem(me_g - d + groups, groups)
        here = omega_half(g, core, omega_owners)
        return remote(here, here, omega_sem.at[d - 1, 1, 0], omega_sem.at[d - 1, 1, 1], sibling)

    with jax.named_scope("omega_b"):
        for d in range(1, groups):
            g = lax.rem(me_g - d + groups, groups)
            gather_finish(
                omega_half(g, core, omega_owners), omega_half(g, core, omega_owners - 1),
                proj_strips.at[pl.ds(0, chips - 1), 0, pl.ds(0, omega_strip)],
                omega_sem.at[d - 1, 0], omega_owners,
            )
            omega_pair(d).start()
    def omega_finish():
        for d in range(1, groups):
            omega_pair(d).wait_recv()
        for g in range(groups):
            omega_high[g], omega_low[g] = split(omega[g])

    def own_row(p, g, up):
        return g * seg + jnp.where(up, p, seg - 1 - p)

    def back(p, d):
        y = own_row(p, me_g, upward)
        here = sketch.at[y]
        at = y - me_g * seg
        return remote(here, here, back_send.at[d - 1, at], back_recv.at[d - 1, at], device(other_group(d), me_b))

    def back_start(lo, hi):
        for p in order[lo:hi]:
            for d in range(1, groups):
                back(p, d).start()

    def store_row(y):
        pltpu.make_async_copy(sketch.at[y], sketch_out.at[y], out_sem).start()

    def columns_of(rows, d):
        ys = [own_row(p, me_g, upward) for p in rows]
        blocks = [grown[y] if d == 0 else cross[d - 1, y - me_g * seg] for y in ys]
        blocks = [block.reshape(slab * span_z, cols) for block in blocks]
        return split(jnp.concatenate(blocks, axis=0) if len(blocks) > 1 else blocks[0])

    def sketch_batch(rows, start):
        for p in rows:
            at = own_row(p, me_g, upward) - me_g * seg
            for d in range(1, groups):
                here = cross.at[d - 1, at]
                remote(here, here, row_send.at[0], row_recv.at[d - 1, at], sibling).wait_recv()
        value = None
        for d in range(groups):
            g = lax.rem(me_g - d + groups, groups)
            term = parts_dot(columns_of(rows, d), (omega_high[g], omega_low[g]), ((1,), (0,)))
            value = term if value is None else value + term
        size = slab * span_z
        for k, p in enumerate(rows):
            y = own_row(p, me_g, upward)
            sketch[y] = value[k * size : (k + 1) * size].reshape(slab, span_z, rank)
            store_row(y)
        high, low = split(value)
        term, mixed = pass_dot(high, high, ((0,), (0,))), pass_dot(high, low, ((0,), (0,)))
        if start:
            gram[...], gram_mixed[...] = term, mixed
        else:
            gram[...] += term
            gram_mixed[...] += mixed

    def project_batch(rows, start):
        blocks = [sketch[own_row(p, me_g, upward)].reshape(slab * span_z, rank) for p in rows]
        value = split(jnp.concatenate(blocks, axis=0) if len(blocks) > 1 else blocks[0])
        for d in range(groups):
            g = lax.rem(me_g - d + groups, groups)
            term = parts_dot(value, columns_of(rows, d), ((0,), (0,)))
            if start:
                proj[g] = term
            else:
                proj[g] += term

    cutoff = plan[0][0]
    lax.fori_loop(2 * middle, cutoff, body, 0)
    with jax.named_scope("omega_c"):
        omega_finish()
    done = 0
    for i in range(cutoff, span_y):
        with jax.named_scope("late_row"):
            if i < chunks:
                halo_wait(i)
            if i + 1 < span_y:
                first_row(i + 1)
            step(i)
            if i + WINDOW < chunks:
                halo_start(i + WINDOW)
        while done < len(plan) and plan[done][0] == i:
            rows = plan[done][1]
            with jax.named_scope("sketch"):
                sketch_batch(rows, done == 0)
            if i < span_y - 1:
                with jax.named_scope("project"):
                    project_batch(rows, done == 0)
            done += 1
            if done == 2:
                back_start(0, FIRST_BACK)
    late = [(k, rows) for k, (i, rows) in enumerate(plan) if i == span_y - 1]

    half = pl.ds(pl.multiple_of(core * half_packed, 8), half_packed)
    far_half = pl.ds(pl.multiple_of((1 - core) * half_packed, 8), half_packed)
    gram[...] += gram_mixed[...] + gram_mixed[...].T
    for k, (i, j) in enumerate(tiles(rank)):
        packed[k * LANES : (k + 1) * LANES] = gram[i * LANES : (i + 1) * LANES, j * LANES : (j + 1) * LANES]
    gram_pair = remote(packed.at[far_half], gram_rx, gram_sem.at[0, 0], gram_sem.at[0, 1], sibling)
    gram_pair.start()
    with jax.named_scope("project_late"):
        for k, rows in late:
            project_batch(rows, k == 0)
    proj_half = pl.ds(pl.multiple_of(core * (rank // 2), 8), rank // 2)
    proj_far = pl.ds(pl.multiple_of((1 - core) * (rank // 2), 8), rank // 2)
    proj_pair = remote(proj.at[:, proj_far], proj_rx, proj_sem.at[0, 0], proj_sem.at[0, 1], sibling)
    proj_pair.start()

    def scatter(source, at, sink, sem, owners):
        def one(d, carry):
            o = chip_peer(d)

            def send():
                remote(at(source, o), sink.at[chip], sem.at[0], sem.at[1], device(me_g, o * 2 + core)).start()

            guarded(owners, o, send)
            return carry

        lax.fori_loop(1, chips, one, 0)

    def scatter_sum(source, at, sink, sem, owners, result):
        def receive():
            bytes_wait(sink.at[pl.ds(0, chips - 1)], sem.at[1])
            sink[chip] = at(source, chip)[...]
            total = sink[0]
            for o in range(1, chips):
                total = total + sink[o]
            result(total)

        guarded(owners, chip, receive)

    def scatter_sent(sink, sem, owners):
        if owners == chips:
            bytes_wait(sink.at[pl.ds(0, owners - 1)], sem.at[0])
        else:
            @pl.when(chip < owners)
            def _():
                bytes_wait(sink.at[pl.ds(0, owners - 1)], sem.at[0])

            @pl.when(chip >= owners)
            def _():
                bytes_wait(sink.at[pl.ds(0, owners)], sem.at[0])

    def gram_at(ref, o):
        return ref.at[pl.ds(pl.multiple_of(core * half_packed + o * gram_strip, 8), gram_strip)]

    def proj_at(ref, o):
        return ref.at[:, pl.ds(pl.multiple_of(core * (rank // 2) + o * proj_strip_rows, 8), proj_strip_rows)]

    def full_at(ref, o):
        return ref.at[pl.ds(pl.multiple_of(core * (rank // 2) + o * proj_strip_rows, 8), proj_strip_rows)]

    with jax.named_scope("gram_pair"):
        gram_pair.wait_recv()
    packed[half] += gram_rx[...]
    scatter(packed, gram_at, gram_strips, gram_sem.at[1], gram_owners)
    def gram_cross(d):
        return remote(
            gram_y.at[me_g], gram_y.at[me_g],
            gram_sem.at[2 + d, 0], gram_sem.at[2 + d, 1], device(other_group(d), me_b),
        )

    def gram_cross_start(total):
        gram_y[me_g] = total
        for d in range(1, groups):
            gram_cross(d).start()

    with jax.named_scope("gram_scatter"):
        scatter_sum(packed, gram_at, gram_strips, gram_sem.at[1], gram_owners, gram_cross_start)
    back_start(FIRST_BACK, SECOND_BACK)

    def proj_cross(d):
        g = other_group(d)
        return remote(
            proj_strip.at[g], proj_y.at[me_g],
            proj_sem.at[2 + d, 0], proj_sem.at[2 + d, 1], device(g, me_b),
        )

    def proj_cross_start(total):
        proj_strip[...] = total
        proj_y[me_g] = proj_strip[me_g]
        for d in range(1, groups):
            proj_cross(d).start()

    with jax.named_scope("proj_pair"):
        proj_pair.wait_recv()
    proj[:, proj_half] += proj_rx[...]

    def gram_cross_finish():
        for d in range(1, groups):
            gram_cross(d).wait_recv()
        total = gram_y[0]
        for g in range(1, groups):
            total = total + gram_y[g]
        gram_at(gram_full, chip)[...] = total

    scatter_sent(gram_strips, gram_sem.at[1], gram_owners)
    with jax.named_scope("gram_cross"):
        guarded(gram_owners, chip, gram_cross_finish)
    gather_start(gram_full, gram_at, gram_sem.at[2], gram_owners)
    with jax.named_scope("gram_gather"):
        base = pl.multiple_of(core * half_packed, 8)
        gather_finish(
            gram_full.at[half], gram_full.at[pl.ds(base, gram_strip * (gram_owners - 1))],
            gram_strips.at[pl.ds(0, chips - 1)], gram_sem.at[2], gram_owners,
        )
    gram_pair.wait_send()
    gram_join = remote(gram_full.at[half], gram_full.at[half], gram_sem.at[2 + groups, 0], gram_sem.at[2 + groups, 1], sibling)
    gram_join.start()
    scatter(proj, proj_at, proj_strips, proj_sem.at[1], proj_owners)
    row = lax.broadcasted_iota(jnp.int32, (rank, rank), 0)
    col = lax.broadcasted_iota(jnp.int32, (rank, rank), 1)
    both[:, rank:] = jnp.where(row == col, 1.0, 0.0)
    both[:, 0:rank] = jnp.zeros((rank, rank), jnp.float32)
    with jax.named_scope("gram_join"):
        gram_join.wait_recv()
    for k, (i, j) in enumerate(tiles(rank)):
        both[i * LANES : (i + 1) * LANES, j * LANES : (j + 1) * LANES] = gram_full[k * LANES : (k + 1) * LANES]

    def proj_cross_finish():
        for d in range(1, groups):
            proj_cross(d).wait_recv()
        total = proj_y[0]
        for g in range(1, groups):
            total = total + proj_y[g]
        full_at(proj_full, chip)[...] = total

    proj_join = remote(
        proj_full.at[proj_half], proj_full.at[proj_half],
        proj_sem.at[2 + groups, 0], proj_sem.at[2 + groups, 1], sibling,
    )

    def hook_scatter():
        with jax.named_scope("proj_scatter"):
            scatter_sum(proj, proj_at, proj_strips, proj_sem.at[1], proj_owners, proj_cross_start)
        back_start(SECOND_BACK, seg)

    def hook_cross():
        with jax.named_scope("proj_cross"):
            scatter_sent(proj_strips, proj_sem.at[1], proj_owners)
            guarded(proj_owners, chip, proj_cross_finish)
            gather_start(proj_full, full_at, proj_sem.at[2], proj_owners)

    def hook_gather():
        with jax.named_scope("proj_gather"):
            base = pl.multiple_of(core * (rank // 2), 8)
            gather_finish(
                proj_full.at[proj_half], proj_full.at[pl.ds(base, proj_strip_rows * (proj_owners - 1))],
                proj_strips.at[pl.ds(0, chips - 1), 0], proj_sem.at[2], proj_owners,
            )
            proj_pair.wait_send()
            proj_join.start()

    blocks = rank // BLOCK
    row = lax.broadcasted_iota(jnp.int32, (BLOCK, LANES), 0)
    prev, prev_left, prev_right = None, 0, 0
    for block in range(blocks):
        if block == HOOK_SCATTER:
            hook_scatter()
        if block == HOOK_CROSS:
            hook_cross()
        at = block * BLOCK
        scope = jax.named_scope("factor")
        scope.__enter__()
        left = at // LANES * LANES
        right = rank + -(-(at + BLOCK) // LANES) * LANES
        panel = both[at : at + BLOCK, left:right]
        if block > 0:
            turned = prev[:, left - prev_left : left - prev_left + LANES].T
            off = at - left
            near = dot(turned[off : off + BLOCK], prev[:, left - prev_left :], ((1,), (0,)))
            common = prev_right - left
            updated = panel[:, :common] - near
            panel = jnp.concatenate([updated, panel[:, common:]], axis=1) if common < right - left else updated
            if off + BLOCK < LANES:
                rest = dot(turned[off + BLOCK :], prev[:, left - prev_left :], ((1,), (0,)))
                both[at + BLOCK : left + LANES, left:prev_right] -= rest
            if left + LANES < rank:
                far = dot(prev[:, left - prev_left + LANES : rank - prev_left], prev[:, left - prev_left + LANES :], ((0,), (0,)))
                both[left + LANES : rank, left + LANES : prev_right] -= far
        pivots = jnp.ones((BLOCK, LANES), jnp.float32)
        for base in range(0, BLOCK, GROUP):
            columns = [
                jnp.broadcast_to(panel[:, at - left + j : at - left + j + 1], (BLOCK, LANES))
                for j in range(base, base + GROUP)
            ]
            for t in range(GROUP):
                j = base + t
                pivot = columns[t][j : j + 1, :]
                over = 1.0 / pivot
                pivots = jnp.where(row == j, pivot, pivots)
                factor = jnp.where(row > j, columns[t], 0.0)
                for u in range(t + 1, GROUP):
                    columns[u] = columns[u] - factor * (columns[u][j : j + 1, :] * over)
                pieces = [
                    panel[:, w : w + LANES] - factor * (panel[j : j + 1, w : w + LANES] * over)
                    for w in range(0, right - left, LANES)
                ]
                panel = jnp.concatenate(pieces, axis=1)
        scale = lax.rsqrt(pivots)
        prev = jnp.concatenate([panel[:, w : w + LANES] * scale for w in range(0, right - left, LANES)], axis=1)
        prev_left, prev_right = left, right
        both[at : at + BLOCK, left:right] = prev
        scope.__exit__(None, None, None)

    pltpu.make_async_copy(both.at[:, pl.ds(rank, rank)], inverse_out, local_sem.at[0]).start()
    hook_gather()
    with jax.named_scope("proj_join"):
        proj_join.wait_recv()
    pltpu.make_async_copy(proj_full, proj_out, local_sem.at[1]).start()
    with jax.named_scope("rows_back"):
        for d in range(1, groups):
            g = lax.rem(me_g - d + groups, groups)
            for p in order:
                y = own_row(p, g, g >= groups // 2)
                here = sketch.at[y]
                remote(here, here, back_send.at[0, 0], back_recv.at[d - 1, y - g * seg], sibling).wait_recv()
                store_row(y)
    with jax.named_scope("finish"):
        pltpu.make_async_copy(both.at[:, pl.ds(rank, rank)], inverse_out, local_sem.at[0]).wait()
        pltpu.make_async_copy(proj_full, proj_out, local_sem.at[1]).wait()
        pltpu.make_async_copy(sketch, sketch_out, out_sem).wait()

    def sent(k, carry):
        @pl.when(me_b < bricks - 1)
        def _():
            halo(k, True).wait_send()

        @pl.when(me_b > 0)
        def _():
            halo(k, False).wait_send()

        return carry

    with jax.named_scope("sends"):
        sent(0, 0)
        lax.fori_loop(1, chunks, sent, 0)

        def row_sent(y, carry):
            @pl.when(y // seg != me_g)
            def _():
                row_copy(y, y // seg).wait_send()

            return carry

        lax.fori_loop(0, span_y, row_sent, 0)
        for d in range(1, groups):
            for p in order:
                back(p, d).wait_send()
            guarded(omega_owners, chip, lambda: spread(d).wait_send())
            omega_pair(d).wait_send()
            guarded(gram_owners, chip, lambda: gram_cross(d).wait_send())
            guarded(proj_owners, chip, lambda: proj_cross(d).wait_send())
        gram_join.wait_send()
        proj_join.wait_send()


def finish_kernel(
    scale, sketch_hbm, inverse_hbm, crossed_hbm, basis, projected,
    sketch, inverse, crossed, staged, result, load_sem, out_sem,
):
    span_y, slab, span_z, rank = sketch.shape
    count = span_y // PIECES
    loads = [
        pltpu.make_async_copy(inverse_hbm, inverse, load_sem.at[0]),
        pltpu.make_async_copy(crossed_hbm, crossed, load_sem.at[1]),
    ]
    for k in range(PIECES):
        at = pl.ds(k * count, count)
        loads.append(pltpu.make_async_copy(sketch_hbm.at[at], sketch.at[at], load_sem.at[2 + k]))
    for load in loads:
        load.start()
    with jax.named_scope("k2_wait"):
        loads[0].wait()
    weights = split(inverse[...])
    turned = split((inverse[...] * scale).T)
    stores = []
    for k in range(PIECES):
        with jax.named_scope("k2_load"):
            loads[2 + k].wait()
        left = split(sketch[k * count : (k + 1) * count].reshape(count * slab * span_z, rank))
        value = parts_dot(left, turned, ((1,), (0,))).reshape(count, slab, span_z, rank)
        for j in range(count):
            staged[:, k * count + j] = value[j]
        at = pl.ds(k * count, count)
        stores.append(pltpu.make_async_copy(staged.at[:, at], basis.at[:, at], out_sem.at[k]))
        stores[-1].start()
    with jax.named_scope("k2_load"):
        loads[1].wait()
    result[...] = parts_dot(weights, split(crossed[...]), ((1,), (0,)))
    stores.append(pltpu.make_async_copy(result, projected, out_sem.at[PIECES]))
    stores[-1].start()
    with jax.named_scope("k2_store"):
        for store in stores:
            store.wait()


def finish(cells, slab, sketch, inverse, crossed):
    span_y, slab, span_z, rank = sketch.shape
    cols = crossed.shape[1]
    vmem = lambda *shape: pltpu.VMEM(shape, jnp.float32)
    return pl.pallas_call(
        functools.partial(finish_kernel, float(cells) ** 0.5),
        out_shape=(
            jax.ShapeDtypeStruct((slab, span_y, span_z, rank), jnp.float32),
            jax.ShapeDtypeStruct((rank, cols), jnp.float32),
        ),
        in_specs=[pl.BlockSpec(memory_space=pl.ANY)] * 3,
        out_specs=[pl.BlockSpec(memory_space=pl.ANY)] * 2,
        scratch_shapes=[
            vmem(span_y, slab, span_z, rank),
            vmem(rank, rank),
            vmem(rank, cols),
            vmem(slab, span_y, span_z, rank),
            vmem(rank, cols),
            pltpu.SemaphoreType.DMA((2 + PIECES,)),
            pltpu.SemaphoreType.DMA((1 + PIECES,)),
        ],
        compiler_params=pltpu.CompilerParams(vmem_limit_bytes=60 * 1024 * 1024),
    )(sketch, inverse, crossed)


def shards(groups, bricks, low_factor, test_matrix):
    slab, span_y, span_z, cols = low_factor.shape
    rank = test_matrix.shape[1]
    cells = bricks * slab * span_y * span_z
    chips = bricks // 2
    seg = span_y // groups
    chunks = span_y - LEAD + 1
    total = packed_rows(rank)
    gram_strip = total // 2 // share(total // 2, chips)
    proj_strip = rank // 2 // share(rank // 2, chips)
    vmem = lambda *shape: pltpu.VMEM(shape, jnp.float32)
    dma = pltpu.SemaphoreType.DMA
    sketch, inverse, crossed = pl.pallas_call(
        functools.partial(kernel, (groups, bricks, slab, span_y, span_z, cells)),
        out_shape=(
            jax.ShapeDtypeStruct((span_y, slab, span_z, rank), jnp.float32),
            jax.ShapeDtypeStruct((rank, rank), jnp.float32),
            jax.ShapeDtypeStruct((rank, cols), jnp.float32),
        ),
        in_specs=[pl.BlockSpec(memory_space=pl.ANY)] * 2,
        out_specs=[pl.BlockSpec(memory_space=pl.ANY)] * 3,
        scratch_shapes=[
            vmem(groups, cols, rank),
            pltpu.VMEM((groups, cols, rank), jnp.bfloat16),
            pltpu.VMEM((groups, cols, rank), jnp.bfloat16),
            vmem(slab + 4, span_y + 2, span_z, cols),
            vmem(slab + 2, span_y + 2, span_z, cols),
            vmem(span_y, slab, span_z, cols),
            vmem(groups - 1, seg, slab, span_z, cols),
            vmem(span_y, slab, span_z, rank),
            vmem(rank, rank),
            vmem(rank, rank),
            vmem(total, LANES),
            vmem(total // 2, LANES),
            vmem(chips, gram_strip, LANES),
            vmem(groups, gram_strip, LANES),
            vmem(total, LANES),
            vmem(groups, rank, cols),
            vmem(groups, rank // 2, cols),
            vmem(chips, groups, proj_strip, cols),
            vmem(groups, proj_strip, cols),
            vmem(groups, proj_strip, cols),
            vmem(rank, cols),
            vmem(rank, 2 * rank),
            dma((2,)),
            dma,
            dma((2, chunks)),
            dma((2, chunks)),
            dma((span_y,)),
            dma((groups - 1, seg)),
            dma((groups - 1, seg)),
            dma((groups - 1, seg)),
            dma((2, groups - 1)),
            dma((groups - 1, 2, 2)),
            dma((3 + groups, 2)),
            dma((3 + groups, 2)),
        ],
        compiler_params=pltpu.CompilerParams(
            collective_id=0, has_side_effects=True, vmem_limit_bytes=60 * 1024 * 1024
        ),
    )(low_factor, test_matrix)
    return finish(cells, slab, sketch, inverse, crossed)


def solution(mesh):
    return jax.shard_map(
        functools.partial(shards, mesh.shape["grp"], mesh.shape["brick"]),
        mesh=mesh,
        in_specs=(P("brick", None, None, "grp"), P("grp", None)),
        out_specs=(P("brick", None, None, None), P(None, "grp")),
        check_vma=False,
    )
```

```python
import functools

import jax
import jax.numpy as jnp
from jax import lax
from jax.experimental import pallas as pl
from jax.experimental.pallas import tpu as pltpu
from jax.sharding import PartitionSpec as P

DIFF = 0.12
CONV = 0.08
MESH = pl.DeviceIdType.MESH
BLOCK = 32
GROUP = 16
LANES = 128
LEAD = 3
OUTER = 4
EARLY = 1
FIRST_BACK = 3
SECOND_BACK = 5
HOOK_CROSS = 3
WRITE = 4


def split(value):
    high = value.astype(jnp.bfloat16)
    return high, (value - high.astype(jnp.float32)).astype(jnp.bfloat16)


def pass_dot(left, right, dims):
    return lax.dot_general(left, right, (dims, ((), ())), preferred_element_type=jnp.float32)


def parts_dot(left, right, dims):
    (ldim,), (rdim,) = dims
    joined = jnp.concatenate([left[0], left[0], left[1]], axis=ldim)
    return pass_dot(joined, jnp.concatenate([right[0], right[1], right[0]], axis=rdim), dims)


def six_parts(value):
    high, _ = split(value)
    rest = value - high.astype(jnp.float32)
    mid, low = split(rest)
    left = jnp.concatenate([high, high, high, mid, mid, low], axis=0)
    return left, jnp.concatenate([high, mid, low, high, mid, high], axis=0)


def outer_product(parts, start, size):
    return pass_dot(parts[0][:, start : start + size], parts[1][:, start:], ((0,), (0,)))


def share(rows, chips):
    return max(k for k in range(1, chips + 1) if rows % (8 * k) == 0)


def batches(groups, seg, span_y):
    if groups != 2 or seg < 4 or seg % 2:
        return [(span_y - 1, [p]) for p in range(seg)]
    mid = seg // 2
    pairs = [[mid + t, mid - 1 - t] for t in range(mid)]
    lead = (mid + 1) // 2
    return [(seg + mid + lead - 1, sum(pairs[:lead], [])), (span_y - 1, sum(pairs[lead:], []))]


def packed_rows(rank):
    blocks = rank // LANES
    return LANES * blocks * (blocks + 1) // 2


def tiles(rank):
    blocks = rank // LANES
    return [(i, j) for i in range(blocks) for j in range(i, blocks)]


def kernel(
    dims, x_hbm, omega_hbm, basis, projected,
    omega, omega_parts, weights, ext, first, grown, cross, sketch, gram, packed, gram_rx, gram_strips,
    gram_y, gram_full, proj, proj_rx, proj_strips, proj_strip, proj_y, proj_full, both,
    local_sem, halo_send, halo_recv, row_send, row_recv, back_send, back_recv,
    spread_sem, omega_sem, gram_sem, proj_sem,
):
    groups, bricks, slab, span_y, span_z, cells = dims
    cols, rank = omega.shape[1:]
    chips = bricks // 2
    seg = span_y // groups
    me_g = lax.axis_index("grp")
    me_b = lax.axis_index("brick")
    chip, core = me_b // 2, lax.rem(me_b, 2)
    upward = me_g >= groups // 2
    chunks = span_y - LEAD + 1
    half_packed = packed_rows(rank) // 2
    gram_owners = share(half_packed, chips)
    gram_strip = half_packed // gram_owners
    proj_owners = share(rank // 2, chips)
    proj_strip_rows = rank // 2 // proj_owners
    omega_owners = share(cols // 2, chips)
    omega_strip = cols // 2 // omega_owners
    plan = batches(groups, seg, span_y)
    order = [p for _, rows in plan for p in rows]

    def device(g, b):
        return {"grp": g, "brick": b}

    def other_group(d):
        return lax.rem(me_g + d, groups)

    def chip_peer(d):
        return lax.rem(chip + d, chips)

    sibling = device(me_g, me_b + 1 - 2 * core)
    barrier = pltpu.get_barrier_semaphore()

    def greet(g, b):
        pl.semaphore_signal(barrier, inc=1, device_id=device(g, b), device_id_type=MESH)

    def remote(source, sink, send, recv, to):
        return pltpu.make_async_remote_copy(
            src_ref=source, dst_ref=sink, send_sem=send, recv_sem=recv,
            device_id=to, device_id_type=MESH,
        )

    def bytes_wait(ref, sem):
        pltpu.make_async_copy(ref, ref, sem).wait()

    outer = jnp.where(core == 0, me_b - 1, me_b + 1)
    has_outer = jnp.logical_and(outer >= 0, outer < bricks)
    with jax.named_scope("greet"):
        for d in range(1, groups):
            greet(other_group(d), me_b)
        lax.fori_loop(1, chips, lambda d, c: (greet(me_g, chip_peer(d) * 2 + core), c)[1], 0)

        @pl.when(has_outer)
        def _():
            greet(me_g, outer)

        greet(me_g, me_b + 1 - 2 * core)

    mine = pltpu.make_async_copy(
        x_hbm, ext.at[pl.ds(2, slab), pl.ds(1, span_y)], local_sem.at[0]
    )
    mine.start()
    test = pltpu.make_async_copy(omega_hbm, omega.at[me_g], local_sem.at[1])
    test.start()
    layer = (span_z, cols)
    for y in (0, span_y + 1):
        ext[:, y] = jnp.zeros((slab + 4,) + layer, jnp.float32)
        first[:, y] = jnp.zeros((slab + 2,) + layer, jnp.float32)

    @pl.when(me_b == 0)
    def _():
        ext[0:2] = jnp.zeros((2, span_y + 2) + layer, jnp.float32)

    @pl.when(me_b == bricks - 1)
    def _():
        ext[slab + 2 :] = jnp.zeros((2, span_y + 2) + layer, jnp.float32)

    with jax.named_scope("barrier"):
        pl.semaphore_wait(barrier, groups - 1 + chips + jnp.where(has_outer, 1, 0))

    def row_at(i, count=1):
        return jnp.where(upward, i, span_y - i - count)

    def columns_half(h):
        return pl.ds(h * (cols // 2), cols // 2)

    def halo(k, up, part=None):
        if part is not None:
            start, rows, columns = row_at(0, LEAD), LEAD, columns_half(part)
            k = part * chunks
        else:
            start, rows, columns = row_at(k + LEAD - 1), 1, pl.ds(0, cols)
        side = 0 if up else 1
        return remote(
            x_hbm.at[pl.ds(slab - 2 if up else 0, 2), pl.ds(start, rows), :, columns],
            ext.at[pl.ds(0 if up else slab + 2, 2), pl.ds(1 + start, rows), :, columns],
            halo_send.at[side, k], halo_recv.at[side, k],
            device(me_g, me_b + 1 if up else me_b - 1),
        )

    def halo_start(k, inner, part=None):
        ways = ((core == 0, True), (core == 1, False))
        for sibling_side, up in ways:
            right = sibling_side if inner else jnp.logical_and(jnp.logical_not(sibling_side), has_outer)

            @pl.when(right)
            def _():
                halo(k, up, part).start()

    def halo_wait(k, part=None):
        @pl.when(me_b > 0)
        def _():
            halo(k, True, part).wait_recv()

        @pl.when(me_b < bricks - 1)
        def _():
            halo(k, False, part).wait_recv()

    for part in range(2):
        halo_start(0, False, part)
        halo_start(0, True, part)
    for k in range(1, min(EARLY + 1, chunks)):
        halo_start(k, False)
    test.wait()

    def omega_at(g, o, c):
        return omega.at[g, pl.ds(pl.multiple_of((c * omega_owners + o) * omega_strip, 8), omega_strip)]

    def spread(d):
        here = omega_at(me_g, chip, core)
        return remote(here, here, spread_sem.at[0, d - 1], spread_sem.at[1, d - 1], device(other_group(d), me_b))

    def guarded(owners, index, action):
        if owners == chips:
            action()
        else:
            pl.when(index < owners)(action)

    def spread_start():
        for d in range(1, groups):
            spread(d).start()

    guarded(omega_owners, chip, spread_start)

    def inward(k, carry):
        halo_start(k, True)
        return carry

    def outward(k, carry):
        halo_start(k, False)
        return carry

    lax.fori_loop(1, chunks, inward, 0)
    mine.wait()

    def operate(mid, low, high, before, after):
        z = lax.broadcasted_iota(jnp.int32, mid.shape, mid.ndim - 2)
        down = jnp.where(z == 0, 0.0, pltpu.roll(mid, 1, mid.ndim - 2))
        up = jnp.where(z == span_z - 1, 0.0, pltpu.roll(mid, span_z - 1, mid.ndim - 2))
        beside = low + high + before + after + down + up
        return mid - DIFF * beside - CONV * (low - high)

    gate_low = jnp.where(me_b == 0, 0.0, 1.0)
    gate_high = jnp.where(me_b == bricks - 1, 0.0, 1.0)

    def first_row(i, cs=slice(None)):
        y = row_at(i)
        for i in range(slab + 2):
            value = operate(
                ext[i + 1, y + 1, :, cs], ext[i, y + 1, :, cs], ext[i + 2, y + 1, :, cs],
                ext[i + 1, y, :, cs], ext[i + 1, y + 2, :, cs],
            )
            if i == 0:
                value = value * gate_low
            if i == slab + 1:
                value = value * gate_high
            first[i, y + 1, :, cs] = value

    def second_row(i, cs=slice(None)):
        y = row_at(i)
        for i in range(slab):
            grown[y, i, :, cs] = operate(
                first[i + 1, y + 1, :, cs], first[i, y + 1, :, cs], first[i + 2, y + 1, :, cs],
                first[i + 1, y, :, cs], first[i + 1, y + 2, :, cs],
            )

    def row_copy(y, owner, columns=pl.ds(0, cols)):
        d = lax.rem(owner - me_g + groups, groups)
        at = y - owner * seg
        return remote(
            grown.at[y, :, :, columns], cross.at[d - 1, at, :, :, columns],
            row_send.at[y], row_recv.at[d - 1, at], device(owner, me_b),
        )

    def send_row(i, columns=pl.ds(0, cols)):
        y = row_at(i)
        owner = y // seg

        @pl.when(owner != me_g)
        def _():
            row_copy(y, owner, columns).start()

    def step(i):
        second_row(i)
        send_row(i)

    def gather_start(buf, at, sem, owners):
        def send():
            def one(d, carry):
                here = at(buf, chip)
                remote(here, here, sem.at[0], sem.at[1], device(me_g, chip_peer(d) * 2 + core)).start()
                return carry

            lax.fori_loop(1, chips, one, 0)

        guarded(owners, chip, send)

    def gather_finish(received, all_but_one, sent, sem, owners):
        if owners == chips:
            bytes_wait(all_but_one, sem.at[1])
            bytes_wait(all_but_one, sem.at[0])
        else:
            @pl.when(chip < owners)
            def _():
                bytes_wait(all_but_one, sem.at[1])
                bytes_wait(sent, sem.at[0])

            @pl.when(chip >= owners)
            def _():
                bytes_wait(received, sem.at[1])

    def omega_half(g, c, strips):
        return omega.at[g, pl.ds(pl.multiple_of(c * (cols // 2), 8), strips * omega_strip)]

    def omega_gather(d):
        g = lax.rem(me_g - d + groups, groups)
        guarded(omega_owners, chip, lambda: spread(d).wait_recv())
        gather_start(omega.at[g], lambda ref, o: ref.at[
            pl.ds(pl.multiple_of((core * omega_owners + o) * omega_strip, 8), omega_strip)
        ], omega_sem.at[d - 1, 0], omega_owners)

    def omega_pair(d):
        g = lax.rem(me_g - d + groups, groups)
        here = omega_half(g, core, omega_owners)
        return remote(here, here, omega_sem.at[d - 1, 1, 0], omega_sem.at[d - 1, 1, 1], sibling)

    for part in range(2):
        with jax.named_scope("halo0"):
            halo_wait(0, part)
        cs = slice(part * (cols // 2), (part + 1) * (cols // 2))
        with jax.named_scope("row0"):
            first_row(0, cs)
            first_row(1, cs)
            second_row(0, cs)
            send_row(0, columns_half(part))
        if part == 0:
            with jax.named_scope("omega_a"):
                for d in range(1, groups):
                    omega_gather(d)
            lax.fori_loop(EARLY + 1, min(OUTER + 1, chunks), outward, 0)

    def body(i, carry):
        halo_wait(i)
        with jax.named_scope("row"):
            first_row(i + 1)
            step(i)

        @pl.when(i + OUTER < chunks)
        def _():
            halo_start(i + OUTER, False)

        return carry

    def omega_finish():
        for d in range(1, groups):
            omega_pair(d).wait_recv()
        for g in range(groups):
            high, low = split(omega[g])
            for k, part in enumerate((high, low, high)):
                omega_parts[g, k * cols : (k + 1) * cols] = part

    def own_row(p, g, up):
        return g * seg + jnp.where(up, p, seg - 1 - p)

    def back(p, d):
        y = own_row(p, me_g, upward)
        here = sketch.at[y]
        at = y - me_g * seg
        return remote(here, here, back_send.at[d - 1, at], back_recv.at[d - 1, at], device(other_group(d), me_b))

    def back_start(lo, hi):
        for p in order[lo:hi]:
            for d in range(1, groups):
                back(p, d).start()

    def rows_of(ref, rows, offset):
        blocks = [ref[own_row(p, me_g, upward) - offset].reshape(slab * span_z, -1) for p in rows]
        return split(jnp.concatenate(blocks, axis=0) if len(blocks) > 1 else blocks[0])

    def columns_of(rows, d):
        return rows_of(grown, rows, 0) if d == 0 else rows_of(cross.at[d - 1], rows, me_g * seg)

    def sketch_batch(rows, start):
        for p in rows:
            at = own_row(p, me_g, upward) - me_g * seg
            for d in range(1, groups):
                here = cross.at[d - 1, at]
                remote(here, here, row_send.at[0], row_recv.at[d - 1, at], sibling).wait_recv()
        left, right = [], []
        for d in range(groups):
            high, low = columns_of(rows, d)
            left += [high, high, low]
            right.append(omega_parts[lax.rem(me_g - d + groups, groups)])
        value = pass_dot(jnp.concatenate(left, axis=1), jnp.concatenate(right, axis=0), ((1,), (0,)))
        size = slab * span_z
        for k, p in enumerate(rows):
            sketch[own_row(p, me_g, upward)] = value[k * size : (k + 1) * size].reshape(slab, span_z, rank)
        high, low = split(value)
        term = pass_dot(high, jnp.concatenate([high, low], axis=1), ((0,), (0,)))
        if start:
            gram[...] = term
        else:
            gram[...] += term

    def project_batch(rows, start):
        value = rows_of(sketch, rows, 0)
        for d in range(groups):
            g = lax.rem(me_g - d + groups, groups)
            term = parts_dot(value, columns_of(rows, d), ((0,), (0,)))
            if start:
                proj[g] = term
            else:
                proj[g] += term

    cutoff = min(plan[0][0], span_y - 3)
    lax.fori_loop(1, cutoff - 1, body, 0)
    with jax.named_scope("omega_b"):
        for d in range(1, groups):
            g = lax.rem(me_g - d + groups, groups)
            gather_finish(
                omega_half(g, core, omega_owners), omega_half(g, core, omega_owners - 1),
                proj_strips.at[pl.ds(0, chips - 1), 0, pl.ds(0, omega_strip)],
                omega_sem.at[d - 1, 0], omega_owners,
            )
            omega_pair(d).start()
    lax.fori_loop(cutoff - 1, cutoff, body, 0)
    done = 0
    for i in range(cutoff, span_y):
        with jax.named_scope("late_row"):
            if i < chunks:
                halo_wait(i)
            if i + 1 < span_y:
                first_row(i + 1)
            step(i)
            if i + OUTER < chunks:
                halo_start(i + OUTER, False)
        if i == cutoff:
            with jax.named_scope("omega_c"):
                omega_finish()
        while done < len(plan) and plan[done][0] == i:
            rows = plan[done][1]
            with jax.named_scope("sketch"):
                sketch_batch(rows, done == 0)
            done += 1
            if done == 1:
                back_start(0, FIRST_BACK)

    half = pl.ds(pl.multiple_of(core * half_packed, 8), half_packed)
    far_half = pl.ds(pl.multiple_of((1 - core) * half_packed, 8), half_packed)
    mixed = gram[:, rank:]
    gram[:, 0:rank] += mixed + mixed.T
    for k, (i, j) in enumerate(tiles(rank)):
        packed[k * LANES : (k + 1) * LANES] = gram[i * LANES : (i + 1) * LANES, j * LANES : (j + 1) * LANES]
    gram_pair = remote(packed.at[far_half], gram_rx, gram_sem.at[0, 0], gram_sem.at[0, 1], sibling)
    gram_pair.start()
    proj_half = pl.ds(pl.multiple_of(core * (rank // 2), 8), rank // 2)
    proj_far = pl.ds(pl.multiple_of((1 - core) * (rank // 2), 8), rank // 2)
    proj_pair = remote(proj.at[:, proj_far], proj_rx, proj_sem.at[0, 0], proj_sem.at[0, 1], sibling)

    def scatter(source, at, sink, sem, owners, lo, hi):
        def one(d, carry):
            o = chip_peer(d)

            def send():
                remote(at(source, o), sink.at[chip], sem.at[0], sem.at[1], device(me_g, o * 2 + core)).start()

            guarded(owners, o, send)
            return carry

        lax.fori_loop(lo, hi, one, 0)

    def scatter_sum(source, at, sink, sem, owners, result):
        def receive():
            bytes_wait(sink.at[pl.ds(0, chips - 1)], sem.at[1])
            sink[chip] = at(source, chip)[...]
            total = sink[0]
            for o in range(1, chips):
                total = total + sink[o]
            result(total)

        guarded(owners, chip, receive)

    def scatter_sent(sink, sem, owners):
        if owners == chips:
            bytes_wait(sink.at[pl.ds(0, owners - 1)], sem.at[0])
        else:
            @pl.when(chip < owners)
            def _():
                bytes_wait(sink.at[pl.ds(0, owners - 1)], sem.at[0])

            @pl.when(chip >= owners)
            def _():
                bytes_wait(sink.at[pl.ds(0, owners)], sem.at[0])

    def gram_at(ref, o):
        return ref.at[pl.ds(pl.multiple_of(core * half_packed + o * gram_strip, 8), gram_strip)]

    def proj_at(ref, o):
        return ref.at[:, pl.ds(pl.multiple_of(core * (rank // 2) + o * proj_strip_rows, 8), proj_strip_rows)]

    def full_at(ref, o):
        return ref.at[pl.ds(pl.multiple_of(core * (rank // 2) + o * proj_strip_rows, 8), proj_strip_rows)]

    with jax.named_scope("project"):
        for k, (i, rows) in enumerate(plan[:-1]):
            project_batch(rows, k == 0)
    with jax.named_scope("gram_pair"):
        gram_pair.wait_recv()
    packed[half] += gram_rx[...]
    scatter(packed, gram_at, gram_strips, gram_sem.at[1], gram_owners, 1, chips)
    with jax.named_scope("project"):
        project_batch(plan[-1][1], len(plan) == 1)
    proj_pair.start()
    with jax.named_scope("proj_pair"):
        proj_pair.wait_recv()
    proj[:, proj_half] += proj_rx[...]
    scatter(proj, proj_at, proj_strips, proj_sem.at[1], proj_owners, 1, chips)

    def gram_cross(d):
        return remote(
            gram_y.at[me_g], gram_y.at[me_g],
            gram_sem.at[2 + d, 0], gram_sem.at[2 + d, 1], device(other_group(d), me_b),
        )

    def gram_cross_start(total):
        gram_y[me_g] = total
        for d in range(1, groups):
            gram_cross(d).start()

    with jax.named_scope("gram_scatter"):
        scatter_sum(packed, gram_at, gram_strips, gram_sem.at[1], gram_owners, gram_cross_start)
    back_start(FIRST_BACK, SECOND_BACK)

    def proj_cross(d):
        g = other_group(d)
        return remote(
            proj_strip.at[g], proj_y.at[me_g],
            proj_sem.at[2 + d, 0], proj_sem.at[2 + d, 1], device(g, me_b),
        )

    def proj_cross_start(total):
        proj_strip[...] = total
        proj_y[me_g] = proj_strip[me_g]
        for d in range(1, groups):
            proj_cross(d).start()


    def gram_cross_finish():
        for d in range(1, groups):
            gram_cross(d).wait_recv()
        total = gram_y[0]
        for g in range(1, groups):
            total = total + gram_y[g]
        gram_at(gram_full, chip)[...] = total

    def sent(k, carry):
        @pl.when(me_b < bricks - 1)
        def _():
            halo(k, True).wait_send()

        @pl.when(me_b > 0)
        def _():
            halo(k, False).wait_send()

        return carry

    def early_sent():
        for part in range(2):
            @pl.when(me_b < bricks - 1)
            def _():
                halo(0, True, part).wait_send()

            @pl.when(me_b > 0)
            def _():
                halo(0, False, part).wait_send()

        lax.fori_loop(1, chunks, sent, 0)

        def row_sent(y, carry):
            @pl.when(y // seg != me_g)
            def _():
                row_copy(y, y // seg).wait_send()

            return carry

        lax.fori_loop(0, span_y, row_sent, 0)
        for d in range(1, groups):
            guarded(omega_owners, chip, lambda: spread(d).wait_send())
            omega_pair(d).wait_send()

    scatter_sent(gram_strips, gram_sem.at[1], gram_owners)
    with jax.named_scope("gram_cross"):
        guarded(gram_owners, chip, gram_cross_finish)
    gather_start(gram_full, gram_at, gram_sem.at[2], gram_owners)
    early_sent()
    with jax.named_scope("gram_gather"):
        base = pl.multiple_of(core * half_packed, 8)
        gather_finish(
            gram_full.at[half], gram_full.at[pl.ds(base, gram_strip * (gram_owners - 1))],
            gram_strips.at[pl.ds(0, chips - 1)], gram_sem.at[2], gram_owners,
        )
    gram_pair.wait_send()
    gram_join = remote(gram_full.at[half], gram_full.at[half], gram_sem.at[2 + groups, 0], gram_sem.at[2 + groups, 1], sibling)
    gram_join.start()
    def proj_cross_finish():
        for d in range(1, groups):
            proj_cross(d).wait_recv()
        total = proj_y[0]
        for g in range(1, groups):
            total = total + proj_y[g]
        full_at(proj_full, chip)[...] = total

    proj_join = remote(
        proj_full.at[proj_half], proj_full.at[proj_half],
        proj_sem.at[2 + groups, 0], proj_sem.at[2 + groups, 1], sibling,
    )

    def hook_scatter():
        with jax.named_scope("proj_scatter"):
            scatter_sum(proj, proj_at, proj_strips, proj_sem.at[1], proj_owners, proj_cross_start)
        back_start(SECOND_BACK, seg)

    def hook_cross():
        with jax.named_scope("proj_cross"):
            scatter_sent(proj_strips, proj_sem.at[1], proj_owners)
            guarded(proj_owners, chip, proj_cross_finish)
            gather_start(proj_full, full_at, proj_sem.at[2], proj_owners)

    def hook_gather():
        with jax.named_scope("proj_gather"):
            base = pl.multiple_of(core * (rank // 2), 8)
            gather_finish(
                proj_full.at[proj_half], proj_full.at[pl.ds(base, proj_strip_rows * (proj_owners - 1))],
                proj_strips.at[pl.ds(0, chips - 1), 0], proj_sem.at[2], proj_owners,
            )
            proj_pair.wait_send()
            proj_join.start()

    row = lax.broadcasted_iota(jnp.int32, (rank, rank), 0)
    col = lax.broadcasted_iota(jnp.int32, (rank, rank), 1)
    both[:, rank:] = jnp.where(row == col, 1.0, 0.0)
    both[:, 0:rank] = jnp.zeros((rank, rank), jnp.float32)
    hook_scatter()
    with jax.named_scope("gram_join"):
        gram_join.wait_recv()
    for k, (i, j) in enumerate(tiles(rank)):
        both[i * LANES : (i + 1) * LANES, j * LANES : (j + 1) * LANES] = gram_full[k * LANES : (k + 1) * LANES]

    blocks = rank // BLOCK
    eight = lax.broadcasted_iota(jnp.int32, (8, LANES), 0)
    prev_parts, prev_left, prev_right = None, 0, 0
    for block in range(blocks):
        if block == HOOK_CROSS:
            hook_cross()
        at = block * BLOCK
        scope = jax.named_scope("factor")
        scope.__enter__()
        left = at // LANES * LANES
        right = rank + -(-(at + BLOCK) // LANES) * LANES
        panel = both[at : at + BLOCK, left:right]
        if block > 0:
            off, first_lane, common = at - left, left - prev_left, prev_right - left
            mine = outer_product(prev_parts, first_lane, LANES)
            updated = panel[:, :common] - mine[off : off + BLOCK]
            panel = jnp.concatenate([updated, panel[:, common:]], axis=1) if common < right - left else updated
            if off + BLOCK < LANES:
                both[at + BLOCK : left + LANES, left:prev_right] -= mine[off + BLOCK :]
            if left + LANES < rank:
                beyond = outer_product(prev_parts, first_lane + LANES, rank - left - LANES)
                both[left + LANES : rank, left + LANES : prev_right] -= beyond
        high, wide = BLOCK // 8, (right - left) // LANES
        rows = [
            [panel[8 * q : 8 * q + 8, w * LANES : (w + 1) * LANES] for w in range(wide)] for q in range(high)
        ]
        pivots = [jnp.ones((8, LANES), jnp.float32) for _ in range(high)]
        for base in range(0, BLOCK, GROUP):
            columns = {}
            for u in range(base, base + GROUP):
                w, lane = divmod(at - left + u, LANES)
                for q in range(u // 8, high):
                    columns[u, q] = jnp.broadcast_to(rows[q][w][:, lane : lane + 1], (8, LANES))
            for j in range(base, base + GROUP):
                top, r = divmod(j, 8)
                pivot = columns[j, top][r : r + 1]
                over = 1.0 / pivot
                pivots[top] = jnp.where(eight == r, pivot, pivots[top])
                factor = {q: columns[j, q] * over for q in range(top, high)}
                factor[top] = jnp.where(eight > r, factor[top], 0.0)
                for u in range(j + 1, base + GROUP):
                    entry = columns[j, u // 8][u % 8 : u % 8 + 1]
                    for q in range(u // 8, high):
                        columns[u, q] = columns[u, q] - factor[q] * entry
                for w in range(wide):
                    entry = rows[top][w][r : r + 1]
                    for q in range(top, high):
                        rows[q][w] = rows[q][w] - factor[q] * entry
        scales = [lax.rsqrt(pivot) for pivot in pivots]
        prev = jnp.concatenate(
            [jnp.concatenate([x * scales[q] for x in rows[q]], axis=1) for q in range(high)], axis=0
        )
        prev_parts = six_parts(prev)
        prev_left, prev_right = left, right
        both[at : at + BLOCK, left:right] = prev
        scope.__exit__(None, None, None)

    high, low = split((both[:, rank:] * float(cells) ** 0.5).T)
    for k, part in enumerate((high, low, high)):
        weights[k * rank : (k + 1) * rank] = part

    def write_rows(ys):
        blocks = [sketch[y].reshape(slab * span_z, rank) for y in ys]
        high, low = split(jnp.concatenate(blocks, axis=0) if len(ys) > 1 else blocks[0])
        value = pass_dot(jnp.concatenate([high, high, low], axis=1), weights[...], ((1,), (0,)))
        size = slab * span_z
        for k, y in enumerate(ys):
            basis[:, y] = value[k * size : (k + 1) * size].reshape(slab, span_z, rank)

    with jax.named_scope("basis_own"):
        write_rows([own_row(p, me_g, upward) for p in order])
    hook_gather()
    def project_final():
        with jax.named_scope("proj_join"):
            proj_join.wait_recv()
        projected[...] = parts_dot(split(both[:, rank:]), split(proj_full[...]), ((1,), (0,)))

    with jax.named_scope("rows_back"):
        for d in range(1, groups):
            g = lax.rem(me_g - d + groups, groups)
            first_part = max(len(order) - WRITE, 0)
            parts = [order[:first_part]] * (first_part > 0) + [rows for _, rows in plan if rows[0] in order[first_part:]]
            for k, rows in enumerate(parts):
                if d == groups - 1 and k == len(parts) - 1:
                    project_final()
                ys = [own_row(p, g, g >= groups // 2) for p in rows]
                with jax.named_scope("row_wait"):
                    for y in ys:
                        here = sketch.at[y]
                        remote(here, here, back_send.at[0, 0], back_recv.at[d - 1, y - g * seg], sibling).wait_recv()
                write_rows(ys)

    with jax.named_scope("sends"):
        for d in range(1, groups):
            for p in order:
                back(p, d).wait_send()
            guarded(gram_owners, chip, lambda: gram_cross(d).wait_send())
            guarded(proj_owners, chip, lambda: proj_cross(d).wait_send())
        gram_join.wait_send()
        proj_join.wait_send()


def shards(groups, bricks, low_factor, test_matrix):
    slab, span_y, span_z, cols = low_factor.shape
    rank = test_matrix.shape[1]
    cells = bricks * slab * span_y * span_z
    chips = bricks // 2
    seg = span_y // groups
    chunks = span_y - LEAD + 1
    total = packed_rows(rank)
    gram_strip = total // 2 // share(total // 2, chips)
    proj_strip = rank // 2 // share(rank // 2, chips)
    vmem = lambda *shape: pltpu.VMEM(shape, jnp.float32)
    dma = pltpu.SemaphoreType.DMA
    return pl.pallas_call(
        functools.partial(kernel, (groups, bricks, slab, span_y, span_z, cells)),
        out_shape=(
            pltpu.VMEM((slab, span_y, span_z, rank), jnp.float32),
            pltpu.VMEM((rank, cols), jnp.float32),
        ),
        in_specs=[pl.BlockSpec(memory_space=pltpu.HBM)] * 2,
        out_specs=[pl.BlockSpec(memory_space=pltpu.VMEM)] * 2,
        scratch_shapes=[
            vmem(groups, cols, rank),
            pltpu.VMEM((groups, 3 * cols, rank), jnp.bfloat16),
            pltpu.VMEM((3 * rank, rank), jnp.bfloat16),
            vmem(slab + 4, span_y + 2, span_z, cols),
            vmem(slab + 2, span_y + 2, span_z, cols),
            vmem(span_y, slab, span_z, cols),
            vmem(groups - 1, seg, slab, span_z, cols),
            vmem(span_y, slab, span_z, rank),
            vmem(rank, 2 * rank),
            vmem(total, LANES),
            vmem(total // 2, LANES),
            vmem(chips, gram_strip, LANES),
            vmem(groups, gram_strip, LANES),
            vmem(total, LANES),
            vmem(groups, rank, cols),
            vmem(groups, rank // 2, cols),
            vmem(chips, groups, proj_strip, cols),
            vmem(groups, proj_strip, cols),
            vmem(groups, proj_strip, cols),
            vmem(rank, cols),
            vmem(rank, 2 * rank),
            dma((2,)),
            dma((2, chunks + 1)),
            dma((2, chunks + 1)),
            dma((span_y,)),
            dma((groups - 1, seg)),
            dma((groups - 1, seg)),
            dma((groups - 1, seg)),
            dma((2, groups - 1)),
            dma((groups - 1, 2, 2)),
            dma((3 + groups, 2)),
            dma((3 + groups, 2)),
        ],
        compiler_params=pltpu.CompilerParams(
            collective_id=0, has_side_effects=True, vmem_limit_bytes=48 * 1024 * 1024
        ),
    )(pltpu.with_memory_space_constraint(low_factor, pltpu.HBM), pltpu.with_memory_space_constraint(test_matrix, pltpu.HBM))


def solution(mesh):
    return jax.shard_map(
        functools.partial(shards, mesh.shape["grp"], mesh.shape["brick"]),
        mesh=mesh,
        in_specs=(P("brick", None, None, "grp"), P("grp", None)),
        out_specs=(P("brick", None, None, None), P(None, "grp")),
        check_vma=False,
    )
```

```python
import functools

import jax
import jax.numpy as jnp
from jax import lax
from jax.experimental import pallas as pl
from jax.experimental.pallas import tpu as pltpu
from jax.sharding import PartitionSpec as P

DIFF = 0.12
CONV = 0.08
MESH = pl.DeviceIdType.MESH
BLOCK = 32
GROUP = 16
LANES = 128
LEAD = 3
OUTER = 4
EARLY = 2
INNER = 6
FIRST_BACK = 3
SECOND_BACK = 5
HOOK_CROSS = 3
WRITE = 4


def split(value):
    high = value.astype(jnp.bfloat16)
    return high, (value - high.astype(jnp.float32)).astype(jnp.bfloat16)


def pass_dot(left, right, dims):
    return lax.dot_general(left, right, (dims, ((), ())), preferred_element_type=jnp.float32)


def parts_dot(left, right, dims):
    (ldim,), (rdim,) = dims
    joined = jnp.concatenate([left[0], left[0], left[1]], axis=ldim)
    return pass_dot(joined, jnp.concatenate([right[0], right[1], right[0]], axis=rdim), dims)


def six_parts(value):
    high, _ = split(value)
    rest = value - high.astype(jnp.float32)
    mid, low = split(rest)
    left = jnp.concatenate([high, high, high, mid, mid, low], axis=0)
    return left, jnp.concatenate([high, mid, low, high, mid, high], axis=0)


def outer_product(parts, start, size):
    return pass_dot(parts[0][:, start : start + size], parts[1][:, start:], ((0,), (0,)))


def share(rows, chips):
    return max(k for k in range(1, chips + 1) if rows % (8 * k) == 0)


def batches(groups, seg, span_y):
    if groups != 2 or seg < 4 or seg % 2:
        return [(span_y - 1, [p]) for p in range(seg)]
    mid = seg // 2
    pairs = [[mid + t, mid - 1 - t] for t in range(mid)]
    lead = (mid + 1) // 2
    return [(seg + mid + lead - 1, sum(pairs[:lead], [])), (span_y - 1, sum(pairs[lead:], []))]


def packed_rows(rank):
    blocks = rank // LANES
    return LANES * blocks * (blocks + 1) // 2


def tiles(rank):
    blocks = rank // LANES
    return [(i, j) for i in range(blocks) for j in range(i, blocks)]


def kernel(
    dims, x_hbm, omega_hbm, basis, projected,
    omega, omega_parts, weights, ext, first, grown, cross, sketch, gram, packed, gram_rx, gram_strips,
    gram_y, gram_full, proj, proj_rx, proj_strips, proj_strip, proj_y, proj_full, both,
    local_sem, halo_send, halo_recv, row_send, row_recv, back_send, back_recv,
    spread_sem, omega_sem, gram_sem, proj_sem,
):
    groups, bricks, slab, span_y, span_z, cells = dims
    cols, rank = omega.shape[1:]
    chips = bricks // 2
    seg = span_y // groups
    me_g = lax.axis_index("grp")
    me_b = lax.axis_index("brick")
    chip, core = me_b // 2, lax.rem(me_b, 2)
    upward = me_g >= groups // 2
    chunks = span_y - LEAD + 1
    half_packed = packed_rows(rank) // 2
    gram_owners = share(half_packed, chips)
    gram_strip = half_packed // gram_owners
    proj_owners = share(rank // 2, chips)
    proj_strip_rows = rank // 2 // proj_owners
    omega_owners = share(cols // 2, chips)
    omega_strip = cols // 2 // omega_owners
    plan = batches(groups, seg, span_y)
    order = [p for _, rows in plan for p in rows]

    def device(g, b):
        return {"grp": g, "brick": b}

    def other_group(d):
        return lax.rem(me_g + d, groups)

    def chip_peer(d):
        return lax.rem(chip + d, chips)

    sibling = device(me_g, me_b + 1 - 2 * core)
    barrier = pltpu.get_barrier_semaphore()

    def greet(g, b):
        pl.semaphore_signal(barrier, inc=1, device_id=device(g, b), device_id_type=MESH)

    def remote(source, sink, send, recv, to):
        return pltpu.make_async_remote_copy(
            src_ref=source, dst_ref=sink, send_sem=send, recv_sem=recv,
            device_id=to, device_id_type=MESH,
        )

    def bytes_wait(ref, sem):
        pltpu.make_async_copy(ref, ref, sem).wait()

    outer = jnp.where(core == 0, me_b - 1, me_b + 1)
    has_outer = jnp.logical_and(outer >= 0, outer < bricks)
    with jax.named_scope("greet"):
        for d in range(1, groups):
            greet(other_group(d), me_b)
        lax.fori_loop(1, chips, lambda d, c: (greet(me_g, chip_peer(d) * 2 + core), c)[1], 0)

        @pl.when(has_outer)
        def _():
            greet(me_g, outer)

        greet(me_g, me_b + 1 - 2 * core)

    mine = pltpu.make_async_copy(
        x_hbm, ext.at[pl.ds(2, slab), pl.ds(1, span_y)], local_sem.at[0]
    )
    mine.start()
    test = pltpu.make_async_copy(omega_hbm, omega.at[me_g], local_sem.at[1])
    test.start()
    layer = (span_z, cols)
    for y in (0, span_y + 1):
        ext[:, y] = jnp.zeros((slab + 4,) + layer, jnp.float32)
        first[:, y] = jnp.zeros((slab + 2,) + layer, jnp.float32)

    @pl.when(me_b == 0)
    def _():
        ext[0:2] = jnp.zeros((2, span_y + 2) + layer, jnp.float32)

    @pl.when(me_b == bricks - 1)
    def _():
        ext[slab + 2 :] = jnp.zeros((2, span_y + 2) + layer, jnp.float32)

    with jax.named_scope("barrier"):
        pl.semaphore_wait(barrier, groups - 1 + chips + jnp.where(has_outer, 1, 0))

    def row_at(i, count=1):
        return jnp.where(upward, i, span_y - i - count)

    def columns_half(h):
        return pl.ds(h * (cols // 2), cols // 2)

    def halo(k, up, part=None):
        if part is not None:
            start, rows, columns = row_at(0, LEAD), LEAD, columns_half(part)
            k = part * chunks
        else:
            start, rows, columns = row_at(k + LEAD - 1), 1, pl.ds(0, cols)
        side = 0 if up else 1
        return remote(
            x_hbm.at[pl.ds(slab - 2 if up else 0, 2), pl.ds(start, rows), :, columns],
            ext.at[pl.ds(0 if up else slab + 2, 2), pl.ds(1 + start, rows), :, columns],
            halo_send.at[side, k], halo_recv.at[side, k],
            device(me_g, me_b + 1 if up else me_b - 1),
        )

    def halo_start(k, inner, part=None):
        ways = ((core == 0, True), (core == 1, False))
        for sibling_side, up in ways:
            right = sibling_side if inner else jnp.logical_and(jnp.logical_not(sibling_side), has_outer)

            @pl.when(right)
            def _():
                halo(k, up, part).start()

    def halo_wait(k, part=None):
        @pl.when(me_b > 0)
        def _():
            halo(k, True, part).wait_recv()

        @pl.when(me_b < bricks - 1)
        def _():
            halo(k, False, part).wait_recv()

    for part in range(2):
        halo_start(0, False, part)
        halo_start(0, True, part)
    for k in range(1, min(EARLY + 1, chunks)):
        halo_start(k, False)
    test.wait()

    def omega_at(g, o, c):
        return omega.at[g, pl.ds(pl.multiple_of((c * omega_owners + o) * omega_strip, 8), omega_strip)]

    def spread(d):
        here = omega_at(me_g, chip, core)
        return remote(here, here, spread_sem.at[0, d - 1], spread_sem.at[1, d - 1], device(other_group(d), me_b))

    def guarded(owners, index, action):
        if owners == chips:
            action()
        else:
            pl.when(index < owners)(action)

    def spread_start():
        for d in range(1, groups):
            spread(d).start()

    guarded(omega_owners, chip, spread_start)

    def inward(k, carry):
        halo_start(k, True)
        return carry

    def outward(k, carry):
        halo_start(k, False)
        return carry

    lax.fori_loop(1, min(INNER + 1, chunks), inward, 0)
    mine.wait()

    def operate(mid, low, high, before, after):
        z = lax.broadcasted_iota(jnp.int32, mid.shape, mid.ndim - 2)
        down = jnp.where(z == 0, 0.0, pltpu.roll(mid, 1, mid.ndim - 2))
        up = jnp.where(z == span_z - 1, 0.0, pltpu.roll(mid, span_z - 1, mid.ndim - 2))
        beside = low + high + before + after + down + up
        return mid - DIFF * beside - CONV * (low - high)

    gate_low = jnp.where(me_b == 0, 0.0, 1.0)
    gate_high = jnp.where(me_b == bricks - 1, 0.0, 1.0)

    def first_row(i, cs=slice(None)):
        y = row_at(i)
        for i in range(slab + 2):
            value = operate(
                ext[i + 1, y + 1, :, cs], ext[i, y + 1, :, cs], ext[i + 2, y + 1, :, cs],
                ext[i + 1, y, :, cs], ext[i + 1, y + 2, :, cs],
            )
            if i == 0:
                value = value * gate_low
            if i == slab + 1:
                value = value * gate_high
            first[i, y + 1, :, cs] = value

    def second_row(i, cs=slice(None)):
        y = row_at(i)
        for i in range(slab):
            grown[y, i, :, cs] = operate(
                first[i + 1, y + 1, :, cs], first[i, y + 1, :, cs], first[i + 2, y + 1, :, cs],
                first[i + 1, y, :, cs], first[i + 1, y + 2, :, cs],
            )

    def row_copy(y, owner, columns=pl.ds(0, cols)):
        d = lax.rem(owner - me_g + groups, groups)
        at = y - owner * seg
        return remote(
            grown.at[y, :, :, columns], cross.at[d - 1, at, :, :, columns],
            row_send.at[y], row_recv.at[d - 1, at], device(owner, me_b),
        )

    def send_row(i, columns=pl.ds(0, cols)):
        y = row_at(i)
        owner = y // seg

        @pl.when(owner != me_g)
        def _():
            row_copy(y, owner, columns).start()

    def step(i):
        second_row(i)
        send_row(i)

    def gather_start(buf, at, sem, owners):
        def send():
            def one(d, carry):
                here = at(buf, chip)
                remote(here, here, sem.at[0], sem.at[1], device(me_g, chip_peer(d) * 2 + core)).start()
                return carry

            lax.fori_loop(1, chips, one, 0)

        guarded(owners, chip, send)

    def gather_finish(received, all_but_one, sent, sem, owners):
        if owners == chips:
            bytes_wait(all_but_one, sem.at[1])
            bytes_wait(all_but_one, sem.at[0])
        else:
            @pl.when(chip < owners)
            def _():
                bytes_wait(all_but_one, sem.at[1])
                bytes_wait(sent, sem.at[0])

            @pl.when(chip >= owners)
            def _():
                bytes_wait(received, sem.at[1])

    def omega_half(g, c, strips):
        return omega.at[g, pl.ds(pl.multiple_of(c * (cols // 2), 8), strips * omega_strip)]

    def omega_gather(d):
        g = lax.rem(me_g - d + groups, groups)
        guarded(omega_owners, chip, lambda: spread(d).wait_recv())
        gather_start(omega.at[g], lambda ref, o: ref.at[
            pl.ds(pl.multiple_of((core * omega_owners + o) * omega_strip, 8), omega_strip)
        ], omega_sem.at[d - 1, 0], omega_owners)

    def omega_pair(d):
        g = lax.rem(me_g - d + groups, groups)
        here = omega_half(g, core, omega_owners)
        return remote(here, here, omega_sem.at[d - 1, 1, 0], omega_sem.at[d - 1, 1, 1], sibling)

    for part in range(2):
        with jax.named_scope("halo0"):
            halo_wait(0, part)
        cs = slice(part * (cols // 2), (part + 1) * (cols // 2))
        with jax.named_scope("row0"):
            first_row(0, cs)
            first_row(1, cs)
            second_row(0, cs)
            send_row(0, columns_half(part))
        if part == 0:
            with jax.named_scope("omega_a"):
                for d in range(1, groups):
                    omega_gather(d)
            lax.fori_loop(EARLY + 1, min(OUTER + 1, chunks), outward, 0)

    def body(i, carry):
        halo_wait(i)
        with jax.named_scope("row"):
            first_row(i + 1)
            step(i)

        @pl.when(i + OUTER < chunks)
        def _():
            halo_start(i + OUTER, False)

        @pl.when(i + INNER < chunks)
        def _():
            halo_start(i + INNER, True)

        return carry

    def omega_finish():
        for d in range(1, groups):
            omega_pair(d).wait_recv()
        for g in range(groups):
            high, low = split(omega[g])
            for k, part in enumerate((high, low, high)):
                omega_parts[g, k * cols : (k + 1) * cols] = part

    def own_row(p, g, up):
        return g * seg + jnp.where(up, p, seg - 1 - p)

    def back(p, d):
        y = own_row(p, me_g, upward)
        here = sketch.at[y]
        at = y - me_g * seg
        return remote(here, here, back_send.at[d - 1, at], back_recv.at[d - 1, at], device(other_group(d), me_b))

    def back_start(lo, hi):
        for p in order[lo:hi]:
            for d in range(1, groups):
                back(p, d).start()

    def rows_of(ref, rows, offset):
        blocks = [ref[own_row(p, me_g, upward) - offset].reshape(slab * span_z, -1) for p in rows]
        return split(jnp.concatenate(blocks, axis=0) if len(blocks) > 1 else blocks[0])

    def columns_of(rows, d):
        return rows_of(grown, rows, 0) if d == 0 else rows_of(cross.at[d - 1], rows, me_g * seg)

    def sketch_batch(rows, start):
        for p in rows:
            at = own_row(p, me_g, upward) - me_g * seg
            for d in range(1, groups):
                here = cross.at[d - 1, at]
                remote(here, here, row_send.at[0], row_recv.at[d - 1, at], sibling).wait_recv()
        left, right = [], []
        for d in range(groups):
            high, low = columns_of(rows, d)
            left += [high, high, low]
            right.append(omega_parts[lax.rem(me_g - d + groups, groups)])
        value = pass_dot(jnp.concatenate(left, axis=1), jnp.concatenate(right, axis=0), ((1,), (0,)))
        size = slab * span_z
        for k, p in enumerate(rows):
            sketch[own_row(p, me_g, upward)] = value[k * size : (k + 1) * size].reshape(slab, span_z, rank)
        high, low = split(value)
        term = pass_dot(high, jnp.concatenate([high, low], axis=1), ((0,), (0,)))
        if start:
            gram[...] = term
        else:
            gram[...] += term

    def project_batch(rows, start):
        value = rows_of(sketch, rows, 0)
        for d in range(groups):
            g = lax.rem(me_g - d + groups, groups)
            term = parts_dot(value, columns_of(rows, d), ((0,), (0,)))
            if start:
                proj[g] = term
            else:
                proj[g] += term

    cutoff = min(plan[0][0], span_y - 3)
    lax.fori_loop(1, cutoff - 1, body, 0)
    with jax.named_scope("omega_b"):
        for d in range(1, groups):
            g = lax.rem(me_g - d + groups, groups)
            gather_finish(
                omega_half(g, core, omega_owners), omega_half(g, core, omega_owners - 1),
                proj_strips.at[pl.ds(0, chips - 1), 0, pl.ds(0, omega_strip)],
                omega_sem.at[d - 1, 0], omega_owners,
            )
            omega_pair(d).start()
    lax.fori_loop(cutoff - 1, cutoff, body, 0)
    done = 0
    for i in range(cutoff, span_y):
        with jax.named_scope("late_row"):
            if i < chunks:
                halo_wait(i)
            if i + 1 < span_y:
                first_row(i + 1)
            step(i)
            if i + OUTER < chunks:
                halo_start(i + OUTER, False)
            if i + INNER < chunks:
                halo_start(i + INNER, True)
        if i == cutoff:
            with jax.named_scope("omega_c"):
                omega_finish()
        while done < len(plan) and plan[done][0] == i:
            rows = plan[done][1]
            with jax.named_scope("sketch"):
                sketch_batch(rows, done == 0)
            done += 1
            if done == 1:
                back_start(0, FIRST_BACK)

    half = pl.ds(pl.multiple_of(core * half_packed, 8), half_packed)
    far_half = pl.ds(pl.multiple_of((1 - core) * half_packed, 8), half_packed)
    mixed = gram[:, rank:]
    gram[:, 0:rank] += mixed + mixed.T
    for k, (i, j) in enumerate(tiles(rank)):
        packed[k * LANES : (k + 1) * LANES] = gram[i * LANES : (i + 1) * LANES, j * LANES : (j + 1) * LANES]
    gram_pair = remote(packed.at[far_half], gram_rx, gram_sem.at[0, 0], gram_sem.at[0, 1], sibling)
    gram_pair.start()
    proj_half = pl.ds(pl.multiple_of(core * (rank // 2), 8), rank // 2)
    proj_far = pl.ds(pl.multiple_of((1 - core) * (rank // 2), 8), rank // 2)
    proj_pair = remote(proj.at[:, proj_far], proj_rx, proj_sem.at[0, 0], proj_sem.at[0, 1], sibling)

    def scatter(source, at, sink, sem, owners, lo, hi):
        def one(d, carry):
            o = chip_peer(d)

            def send():
                remote(at(source, o), sink.at[chip], sem.at[0], sem.at[1], device(me_g, o * 2 + core)).start()

            guarded(owners, o, send)
            return carry

        lax.fori_loop(lo, hi, one, 0)

    def scatter_sum(source, at, sink, sem, owners, result):
        def receive():
            bytes_wait(sink.at[pl.ds(0, chips - 1)], sem.at[1])
            sink[chip] = at(source, chip)[...]
            total = sink[0]
            for o in range(1, chips):
                total = total + sink[o]
            result(total)

        guarded(owners, chip, receive)

    def scatter_sent(sink, sem, owners):
        if owners == chips:
            bytes_wait(sink.at[pl.ds(0, owners - 1)], sem.at[0])
        else:
            @pl.when(chip < owners)
            def _():
                bytes_wait(sink.at[pl.ds(0, owners - 1)], sem.at[0])

            @pl.when(chip >= owners)
            def _():
                bytes_wait(sink.at[pl.ds(0, owners)], sem.at[0])

    def gram_at(ref, o):
        return ref.at[pl.ds(pl.multiple_of(core * half_packed + o * gram_strip, 8), gram_strip)]

    def proj_at(ref, o):
        return ref.at[:, pl.ds(pl.multiple_of(core * (rank // 2) + o * proj_strip_rows, 8), proj_strip_rows)]

    def full_at(ref, o):
        return ref.at[pl.ds(pl.multiple_of(core * (rank // 2) + o * proj_strip_rows, 8), proj_strip_rows)]

    with jax.named_scope("project"):
        for k, (i, rows) in enumerate(plan[:-1]):
            project_batch(rows, k == 0)
    with jax.named_scope("gram_pair"):
        gram_pair.wait_recv()
    packed[half] += gram_rx[...]
    scatter(packed, gram_at, gram_strips, gram_sem.at[1], gram_owners, 1, chips)
    with jax.named_scope("project"):
        project_batch(plan[-1][1], len(plan) == 1)
    proj_pair.start()
    with jax.named_scope("proj_pair"):
        proj_pair.wait_recv()
    proj[:, proj_half] += proj_rx[...]
    scatter(proj, proj_at, proj_strips, proj_sem.at[1], proj_owners, 1, chips)

    def gram_cross(d):
        return remote(
            gram_y.at[me_g], gram_y.at[me_g],
            gram_sem.at[2 + d, 0], gram_sem.at[2 + d, 1], device(other_group(d), me_b),
        )

    def gram_cross_start(total):
        gram_y[me_g] = total
        for d in range(1, groups):
            gram_cross(d).start()

    with jax.named_scope("gram_scatter"):
        scatter_sum(packed, gram_at, gram_strips, gram_sem.at[1], gram_owners, gram_cross_start)
    back_start(FIRST_BACK, SECOND_BACK)

    def proj_cross(d):
        g = other_group(d)
        return remote(
            proj_strip.at[g], proj_y.at[me_g],
            proj_sem.at[2 + d, 0], proj_sem.at[2 + d, 1], device(g, me_b),
        )

    def proj_cross_start(total):
        proj_strip[...] = total
        proj_y[me_g] = proj_strip[me_g]
        for d in range(1, groups):
            proj_cross(d).start()


    def gram_cross_finish():
        for d in range(1, groups):
            gram_cross(d).wait_recv()
        total = gram_y[0]
        for g in range(1, groups):
            total = total + gram_y[g]
        gram_at(gram_full, chip)[...] = total

    def sent(k, carry):
        @pl.when(me_b < bricks - 1)
        def _():
            halo(k, True).wait_send()

        @pl.when(me_b > 0)
        def _():
            halo(k, False).wait_send()

        return carry

    def early_sent():
        for part in range(2):
            @pl.when(me_b < bricks - 1)
            def _():
                halo(0, True, part).wait_send()

            @pl.when(me_b > 0)
            def _():
                halo(0, False, part).wait_send()

        lax.fori_loop(1, chunks, sent, 0)

        def row_sent(y, carry):
            @pl.when(y // seg != me_g)
            def _():
                row_copy(y, y // seg).wait_send()

            return carry

        lax.fori_loop(0, span_y, row_sent, 0)
        for d in range(1, groups):
            guarded(omega_owners, chip, lambda: spread(d).wait_send())
            omega_pair(d).wait_send()

    scatter_sent(gram_strips, gram_sem.at[1], gram_owners)
    with jax.named_scope("gram_cross"):
        guarded(gram_owners, chip, gram_cross_finish)
    gather_start(gram_full, gram_at, gram_sem.at[2], gram_owners)
    early_sent()
    with jax.named_scope("gram_gather"):
        base = pl.multiple_of(core * half_packed, 8)
        gather_finish(
            gram_full.at[half], gram_full.at[pl.ds(base, gram_strip * (gram_owners - 1))],
            gram_strips.at[pl.ds(0, chips - 1)], gram_sem.at[2], gram_owners,
        )
    gram_pair.wait_send()
    gram_join = remote(gram_full.at[half], gram_full.at[half], gram_sem.at[2 + groups, 0], gram_sem.at[2 + groups, 1], sibling)
    gram_join.start()
    def proj_cross_finish():
        for d in range(1, groups):
            proj_cross(d).wait_recv()
        total = proj_y[0]
        for g in range(1, groups):
            total = total + proj_y[g]
        full_at(proj_full, chip)[...] = total

    proj_join = remote(
        proj_full.at[proj_half], proj_full.at[proj_half],
        proj_sem.at[2 + groups, 0], proj_sem.at[2 + groups, 1], sibling,
    )

    def hook_scatter():
        with jax.named_scope("proj_scatter"):
            scatter_sum(proj, proj_at, proj_strips, proj_sem.at[1], proj_owners, proj_cross_start)
        back_start(SECOND_BACK, seg)

    def hook_cross():
        with jax.named_scope("proj_cross"):
            scatter_sent(proj_strips, proj_sem.at[1], proj_owners)
            guarded(proj_owners, chip, proj_cross_finish)
            gather_start(proj_full, full_at, proj_sem.at[2], proj_owners)

    def hook_gather():
        with jax.named_scope("proj_gather"):
            base = pl.multiple_of(core * (rank // 2), 8)
            gather_finish(
                proj_full.at[proj_half], proj_full.at[pl.ds(base, proj_strip_rows * (proj_owners - 1))],
                proj_strips.at[pl.ds(0, chips - 1), 0], proj_sem.at[2], proj_owners,
            )
            proj_pair.wait_send()
            proj_join.start()

    row = lax.broadcasted_iota(jnp.int32, (rank, rank), 0)
    col = lax.broadcasted_iota(jnp.int32, (rank, rank), 1)
    both[:, rank:] = jnp.where(row == col, 1.0, 0.0)
    both[:, 0:rank] = jnp.zeros((rank, rank), jnp.float32)
    hook_scatter()
    with jax.named_scope("gram_join"):
        gram_join.wait_recv()
    for k, (i, j) in enumerate(tiles(rank)):
        both[i * LANES : (i + 1) * LANES, j * LANES : (j + 1) * LANES] = gram_full[k * LANES : (k + 1) * LANES]

    blocks = rank // BLOCK
    eight = lax.broadcasted_iota(jnp.int32, (8, LANES), 0)
    prev_parts, prev_left, prev_right = None, 0, 0
    for block in range(blocks):
        if block == HOOK_CROSS:
            hook_cross()
        at = block * BLOCK
        scope = jax.named_scope("factor")
        scope.__enter__()
        left = at // LANES * LANES
        right = rank + -(-(at + BLOCK) // LANES) * LANES
        panel = both[at : at + BLOCK, left:right]
        if block > 0:
            off, first_lane, common = at - left, left - prev_left, prev_right - left
            mine = outer_product(prev_parts, first_lane, LANES)
            updated = panel[:, :common] - mine[off : off + BLOCK]
            panel = jnp.concatenate([updated, panel[:, common:]], axis=1) if common < right - left else updated
            if off + BLOCK < LANES:
                both[at + BLOCK : left + LANES, left:prev_right] -= mine[off + BLOCK :]
            if left + LANES < rank:
                beyond = outer_product(prev_parts, first_lane + LANES, rank - left - LANES)
                both[left + LANES : rank, left + LANES : prev_right] -= beyond
        high, wide = BLOCK // 8, (right - left) // LANES
        rows = [
            [panel[8 * q : 8 * q + 8, w * LANES : (w + 1) * LANES] for w in range(wide)] for q in range(high)
        ]
        pivots = [jnp.ones((8, LANES), jnp.float32) for _ in range(high)]
        for base in range(0, BLOCK, GROUP):
            columns = {}
            for u in range(base, base + GROUP):
                w, lane = divmod(at - left + u, LANES)
                for q in range(u // 8, high):
                    columns[u, q] = jnp.broadcast_to(rows[q][w][:, lane : lane + 1], (8, LANES))
            for j in range(base, base + GROUP):
                top, r = divmod(j, 8)
                pivot = columns[j, top][r : r + 1]
                over = 1.0 / pivot
                pivots[top] = jnp.where(eight == r, pivot, pivots[top])
                factor = {q: columns[j, q] * over for q in range(top, high)}
                factor[top] = jnp.where(eight > r, factor[top], 0.0)
                for u in range(j + 1, base + GROUP):
                    entry = columns[j, u // 8][u % 8 : u % 8 + 1]
                    for q in range(u // 8, high):
                        columns[u, q] = columns[u, q] - factor[q] * entry
                for w in range(wide):
                    entry = rows[top][w][r : r + 1]
                    for q in range(top, high):
                        rows[q][w] = rows[q][w] - factor[q] * entry
        scales = [lax.rsqrt(pivot) for pivot in pivots]
        prev = jnp.concatenate(
            [jnp.concatenate([x * scales[q] for x in rows[q]], axis=1) for q in range(high)], axis=0
        )
        prev_parts = six_parts(prev)
        prev_left, prev_right = left, right
        both[at : at + BLOCK, left:right] = prev
        scope.__exit__(None, None, None)

    high, low = split((both[:, rank:] * float(cells) ** 0.5).T)
    for k, part in enumerate((high, low, high)):
        weights[k * rank : (k + 1) * rank] = part

    def write_rows(ys):
        blocks = [sketch[y].reshape(slab * span_z, rank) for y in ys]
        high, low = split(jnp.concatenate(blocks, axis=0) if len(ys) > 1 else blocks[0])
        value = pass_dot(jnp.concatenate([high, high, low], axis=1), weights[...], ((1,), (0,)))
        size = slab * span_z
        for k, y in enumerate(ys):
            basis[:, y] = value[k * size : (k + 1) * size].reshape(slab, span_z, rank)

    with jax.named_scope("basis_own"):
        write_rows([own_row(p, me_g, upward) for p in order])
    def project_final():
        with jax.named_scope("proj_join"):
            proj_join.wait_recv()
        projected[...] = parts_dot(split(both[:, rank:]), split(proj_full[...]), ((1,), (0,)))

    with jax.named_scope("rows_back"):
        for d in range(1, groups):
            g = lax.rem(me_g - d + groups, groups)
            first_part = max(len(order) - WRITE, 0)
            parts = [order[:first_part]] * (first_part > 0) + [rows for _, rows in plan if rows[0] in order[first_part:]]
            for k, rows in enumerate(parts):
                if d == groups - 1 and k == len(parts) - 1:
                    hook_gather()
                ys = [own_row(p, g, g >= groups // 2) for p in rows]
                with jax.named_scope("row_wait"):
                    for y in ys:
                        here = sketch.at[y]
                        remote(here, here, back_send.at[0, 0], back_recv.at[d - 1, y - g * seg], sibling).wait_recv()
                write_rows(ys)
    project_final()

    with jax.named_scope("sends"):
        for d in range(1, groups):
            for p in order:
                back(p, d).wait_send()
            guarded(gram_owners, chip, lambda: gram_cross(d).wait_send())
            guarded(proj_owners, chip, lambda: proj_cross(d).wait_send())
        gram_join.wait_send()
        proj_join.wait_send()


def store_kernel(basis, projected, basis_out, projected_out, sem):
    copies = [pltpu.make_async_copy(projected, projected_out, sem.at[0])]
    for i in range(basis.shape[0]):
        copies.append(pltpu.make_async_copy(basis.at[i], basis_out.at[i], sem.at[1 + i]))
    for copy in copies:
        copy.start()
    for copy in copies:
        copy.wait()


def store(basis, projected):
    return pl.pallas_call(
        store_kernel,
        out_shape=tuple(jax.ShapeDtypeStruct(x.shape, x.dtype) for x in (basis, projected)),
        in_specs=[pl.BlockSpec(memory_space=pltpu.VMEM)] * 2,
        out_specs=[pl.BlockSpec(memory_space=pltpu.HBM)] * 2,
        scratch_shapes=[pltpu.SemaphoreType.DMA((1 + basis.shape[0],))],
    )(
        pltpu.with_memory_space_constraint(basis, pltpu.VMEM),
        pltpu.with_memory_space_constraint(projected, pltpu.VMEM),
    )


def shards(groups, bricks, low_factor, test_matrix):
    slab, span_y, span_z, cols = low_factor.shape
    rank = test_matrix.shape[1]
    cells = bricks * slab * span_y * span_z
    chips = bricks // 2
    seg = span_y // groups
    chunks = span_y - LEAD + 1
    total = packed_rows(rank)
    gram_strip = total // 2 // share(total // 2, chips)
    proj_strip = rank // 2 // share(rank // 2, chips)
    vmem = lambda *shape: pltpu.VMEM(shape, jnp.float32)
    dma = pltpu.SemaphoreType.DMA
    basis, projected = pl.pallas_call(
        functools.partial(kernel, (groups, bricks, slab, span_y, span_z, cells)),
        out_shape=(
            pltpu.VMEM((slab, span_y, span_z, rank), jnp.float32),
            pltpu.VMEM((rank, cols), jnp.float32),
        ),
        in_specs=[pl.BlockSpec(memory_space=pltpu.HBM)] * 2,
        out_specs=[pl.BlockSpec(memory_space=pltpu.VMEM)] * 2,
        scratch_shapes=[
            vmem(groups, cols, rank),
            pltpu.VMEM((groups, 3 * cols, rank), jnp.bfloat16),
            pltpu.VMEM((3 * rank, rank), jnp.bfloat16),
            vmem(slab + 4, span_y + 2, span_z, cols),
            vmem(slab + 2, span_y + 2, span_z, cols),
            vmem(span_y, slab, span_z, cols),
            vmem(groups - 1, seg, slab, span_z, cols),
            vmem(span_y, slab, span_z, rank),
            vmem(rank, 2 * rank),
            vmem(total, LANES),
            vmem(total // 2, LANES),
            vmem(chips, gram_strip, LANES),
            vmem(groups, gram_strip, LANES),
            vmem(total, LANES),
            vmem(groups, rank, cols),
            vmem(groups, rank // 2, cols),
            vmem(chips, groups, proj_strip, cols),
            vmem(groups, proj_strip, cols),
            vmem(groups, proj_strip, cols),
            vmem(rank, cols),
            vmem(rank, 2 * rank),
            dma((2,)),
            dma((2, chunks + 1)),
            dma((2, chunks + 1)),
            dma((span_y,)),
            dma((groups - 1, seg)),
            dma((groups - 1, seg)),
            dma((groups - 1, seg)),
            dma((2, groups - 1)),
            dma((groups - 1, 2, 2)),
            dma((3 + groups, 2)),
            dma((3 + groups, 2)),
        ],
        compiler_params=pltpu.CompilerParams(
            collective_id=0, has_side_effects=True, vmem_limit_bytes=48 * 1024 * 1024
        ),
    )(pltpu.with_memory_space_constraint(low_factor, pltpu.HBM), pltpu.with_memory_space_constraint(test_matrix, pltpu.HBM))
    return store(basis, projected)


def solution(mesh):
    return jax.shard_map(
        functools.partial(shards, mesh.shape["grp"], mesh.shape["brick"]),
        mesh=mesh,
        in_specs=(P("brick", None, None, "grp"), P("grp", None)),
        out_specs=(P("brick", None, None, None), P(None, "grp")),
        check_vma=False,
    )
```

```python
import functools

import jax
import jax.numpy as jnp
from jax import lax
from jax.experimental import pallas as pl
from jax.experimental.pallas import tpu as pltpu
from jax.sharding import PartitionSpec as P

DIFF = 0.12
CONV = 0.08
MESH = pl.DeviceIdType.MESH
BLOCK = 32
GROUP = 16
LANES = 128
LEAD = 3
OUTER = 4
EARLY = 3
INNER = 6
FIRST_BACK = 3
SECOND_BACK = 5
HOOK_CROSS = 3
WRITE = 4


def split(value):
    high = value.astype(jnp.bfloat16)
    return high, (value - high.astype(jnp.float32)).astype(jnp.bfloat16)


def pass_dot(left, right, dims):
    return lax.dot_general(left, right, (dims, ((), ())), preferred_element_type=jnp.float32)


def parts_dot(left, right, dims):
    (ldim,), (rdim,) = dims
    joined = jnp.concatenate([left[0], left[0], left[1]], axis=ldim)
    return pass_dot(joined, jnp.concatenate([right[0], right[1], right[0]], axis=rdim), dims)


def six_parts(value):
    high, _ = split(value)
    rest = value - high.astype(jnp.float32)
    mid, low = split(rest)
    left = jnp.concatenate([high, high, high, mid, mid, low], axis=0)
    return left, jnp.concatenate([high, mid, low, high, mid, high], axis=0)


def outer_product(parts, start, size):
    return pass_dot(parts[0][:, start : start + size], parts[1][:, start:], ((0,), (0,)))


def share(rows, chips):
    return max(k for k in range(1, chips + 1) if rows % (8 * k) == 0)


def batches(groups, seg, span_y):
    if groups != 2 or seg < 4 or seg % 2:
        return [(span_y - 1, [p]) for p in range(seg)]
    mid = seg // 2
    pairs = [[mid + t, mid - 1 - t] for t in range(mid)]
    lead = (mid + 1) // 2
    return [(seg + mid + lead - 1, sum(pairs[:lead], [])), (span_y - 1, sum(pairs[lead:], []))]


def packed_rows(rank):
    blocks = rank // LANES
    return LANES * blocks * (blocks + 1) // 2


def tiles(rank):
    blocks = rank // LANES
    return [(i, j) for i in range(blocks) for j in range(i, blocks)]


def kernel(
    dims, x_hbm, omega_hbm, basis, inverse_out, crossed,
    omega, omega_parts, weights, ext, first, grown, cross, sketch, gram, packed, gram_rx, gram_strips,
    gram_y, gram_full, proj, proj_rx, proj_strips, proj_strip, proj_y, proj_full, both,
    local_sem, halo_send, halo_recv, row_send, row_recv, back_send, back_recv,
    spread_sem, omega_sem, gram_sem, proj_sem,
):
    groups, bricks, slab, span_y, span_z, cells = dims
    cols, rank = omega.shape[1:]
    chips = bricks // 2
    seg = span_y // groups
    me_g = lax.axis_index("grp")
    me_b = lax.axis_index("brick")
    chip, core = me_b // 2, lax.rem(me_b, 2)
    upward = me_g >= groups // 2
    chunks = span_y - LEAD + 1
    half_packed = packed_rows(rank) // 2
    gram_owners = share(half_packed, chips)
    gram_strip = half_packed // gram_owners
    proj_owners = share(rank // 2, chips)
    proj_strip_rows = rank // 2 // proj_owners
    omega_owners = share(cols // 2, chips)
    omega_strip = cols // 2 // omega_owners
    plan = batches(groups, seg, span_y)
    order = [p for _, rows in plan for p in rows]

    def device(g, b):
        return {"grp": g, "brick": b}

    def other_group(d):
        return lax.rem(me_g + d, groups)

    def chip_peer(d):
        return lax.rem(chip + d, chips)

    sibling = device(me_g, me_b + 1 - 2 * core)
    barrier = pltpu.get_barrier_semaphore()

    def greet(g, b):
        pl.semaphore_signal(barrier, inc=1, device_id=device(g, b), device_id_type=MESH)

    def remote(source, sink, send, recv, to):
        return pltpu.make_async_remote_copy(
            src_ref=source, dst_ref=sink, send_sem=send, recv_sem=recv,
            device_id=to, device_id_type=MESH,
        )

    def bytes_wait(ref, sem):
        pltpu.make_async_copy(ref, ref, sem).wait()

    outer = jnp.where(core == 0, me_b - 1, me_b + 1)
    has_outer = jnp.logical_and(outer >= 0, outer < bricks)
    with jax.named_scope("greet"):
        for d in range(1, groups):
            greet(other_group(d), me_b)
        lax.fori_loop(1, chips, lambda d, c: (greet(me_g, chip_peer(d) * 2 + core), c)[1], 0)

        @pl.when(has_outer)
        def _():
            greet(me_g, outer)

        greet(me_g, me_b + 1 - 2 * core)

    mine = pltpu.make_async_copy(
        x_hbm, ext.at[pl.ds(2, slab), pl.ds(1, span_y)], local_sem.at[0]
    )
    mine.start()
    test = pltpu.make_async_copy(omega_hbm, omega.at[me_g], local_sem.at[1])
    test.start()
    layer = (span_z, cols)
    for y in (0, span_y + 1):
        ext[:, y] = jnp.zeros((slab + 4,) + layer, jnp.float32)
        first[:, y] = jnp.zeros((slab + 2,) + layer, jnp.float32)

    @pl.when(me_b == 0)
    def _():
        ext[0:2] = jnp.zeros((2, span_y + 2) + layer, jnp.float32)

    @pl.when(me_b == bricks - 1)
    def _():
        ext[slab + 2 :] = jnp.zeros((2, span_y + 2) + layer, jnp.float32)

    with jax.named_scope("barrier"):
        pl.semaphore_wait(barrier, groups - 1 + chips + jnp.where(has_outer, 1, 0))

    def row_at(i, count=1):
        return jnp.where(upward, i, span_y - i - count)

    def columns_half(h):
        return pl.ds(h * (cols // 2), cols // 2)

    def halo(k, up, part=None):
        if part is not None:
            start, rows, columns = row_at(0, LEAD), LEAD, columns_half(part)
            k = part * chunks
        else:
            start, rows, columns = row_at(k + LEAD - 1), 1, pl.ds(0, cols)
        side = 0 if up else 1
        return remote(
            x_hbm.at[pl.ds(slab - 2 if up else 0, 2), pl.ds(start, rows), :, columns],
            ext.at[pl.ds(0 if up else slab + 2, 2), pl.ds(1 + start, rows), :, columns],
            halo_send.at[side, k], halo_recv.at[side, k],
            device(me_g, me_b + 1 if up else me_b - 1),
        )

    def halo_start(k, inner, part=None):
        ways = ((core == 0, True), (core == 1, False))
        for sibling_side, up in ways:
            right = sibling_side if inner else jnp.logical_and(jnp.logical_not(sibling_side), has_outer)

            @pl.when(right)
            def _():
                halo(k, up, part).start()

    def halo_wait(k, part=None):
        @pl.when(me_b > 0)
        def _():
            halo(k, True, part).wait_recv()

        @pl.when(me_b < bricks - 1)
        def _():
            halo(k, False, part).wait_recv()

    for part in range(2):
        halo_start(0, False, part)
        halo_start(0, True, part)
    for k in range(1, min(EARLY + 1, chunks)):
        halo_start(k, False)
    test.wait()

    def omega_at(g, o, c):
        return omega.at[g, pl.ds(pl.multiple_of((c * omega_owners + o) * omega_strip, 8), omega_strip)]

    def spread(d):
        here = omega_at(me_g, chip, core)
        return remote(here, here, spread_sem.at[0, d - 1], spread_sem.at[1, d - 1], device(other_group(d), me_b))

    def guarded(owners, index, action):
        if owners == chips:
            action()
        else:
            pl.when(index < owners)(action)

    def spread_start():
        for d in range(1, groups):
            spread(d).start()

    guarded(omega_owners, chip, spread_start)

    def inward(k, carry):
        halo_start(k, True)
        return carry

    def outward(k, carry):
        halo_start(k, False)
        return carry

    lax.fori_loop(1, min(INNER + 1, chunks), inward, 0)
    mine.wait()

    def operate(mid, low, high, before, after):
        z = lax.broadcasted_iota(jnp.int32, mid.shape, mid.ndim - 2)
        down = jnp.where(z == 0, 0.0, pltpu.roll(mid, 1, mid.ndim - 2))
        up = jnp.where(z == span_z - 1, 0.0, pltpu.roll(mid, span_z - 1, mid.ndim - 2))
        beside = low + high + before + after + down + up
        return mid - DIFF * beside - CONV * (low - high)

    gate_low = jnp.where(me_b == 0, 0.0, 1.0)
    gate_high = jnp.where(me_b == bricks - 1, 0.0, 1.0)

    def first_row(i, cs=slice(None)):
        y = row_at(i)
        for i in range(slab + 2):
            value = operate(
                ext[i + 1, y + 1, :, cs], ext[i, y + 1, :, cs], ext[i + 2, y + 1, :, cs],
                ext[i + 1, y, :, cs], ext[i + 1, y + 2, :, cs],
            )
            if i == 0:
                value = value * gate_low
            if i == slab + 1:
                value = value * gate_high
            first[i, y + 1, :, cs] = value

    def second_row(i, cs=slice(None)):
        y = row_at(i)
        for i in range(slab):
            grown[y, i, :, cs] = operate(
                first[i + 1, y + 1, :, cs], first[i, y + 1, :, cs], first[i + 2, y + 1, :, cs],
                first[i + 1, y, :, cs], first[i + 1, y + 2, :, cs],
            )

    def row_copy(y, owner, columns=pl.ds(0, cols)):
        d = lax.rem(owner - me_g + groups, groups)
        at = y - owner * seg
        return remote(
            grown.at[y, :, :, columns], cross.at[d - 1, at, :, :, columns],
            row_send.at[y], row_recv.at[d - 1, at], device(owner, me_b),
        )

    def send_row(i, columns=pl.ds(0, cols)):
        y = row_at(i)
        owner = y // seg

        @pl.when(owner != me_g)
        def _():
            row_copy(y, owner, columns).start()

    def step(i):
        second_row(i)
        send_row(i)

    def gather_start(buf, at, sem, owners):
        def send():
            def one(d, carry):
                here = at(buf, chip)
                remote(here, here, sem.at[0], sem.at[1], device(me_g, chip_peer(d) * 2 + core)).start()
                return carry

            lax.fori_loop(1, chips, one, 0)

        guarded(owners, chip, send)

    def gather_finish(received, all_but_one, sent, sem, owners):
        if owners == chips:
            bytes_wait(all_but_one, sem.at[1])
            bytes_wait(all_but_one, sem.at[0])
        else:
            @pl.when(chip < owners)
            def _():
                bytes_wait(all_but_one, sem.at[1])
                bytes_wait(sent, sem.at[0])

            @pl.when(chip >= owners)
            def _():
                bytes_wait(received, sem.at[1])

    def omega_half(g, c, strips):
        return omega.at[g, pl.ds(pl.multiple_of(c * (cols // 2), 8), strips * omega_strip)]

    def omega_gather(d):
        g = lax.rem(me_g - d + groups, groups)
        guarded(omega_owners, chip, lambda: spread(d).wait_recv())
        gather_start(omega.at[g], lambda ref, o: ref.at[
            pl.ds(pl.multiple_of((core * omega_owners + o) * omega_strip, 8), omega_strip)
        ], omega_sem.at[d - 1, 0], omega_owners)

    def omega_pair(d):
        g = lax.rem(me_g - d + groups, groups)
        here = omega_half(g, core, omega_owners)
        return remote(here, here, omega_sem.at[d - 1, 1, 0], omega_sem.at[d - 1, 1, 1], sibling)

    for part in range(2):
        with jax.named_scope("halo0"):
            halo_wait(0, part)
        cs = slice(part * (cols // 2), (part + 1) * (cols // 2))
        with jax.named_scope("row0"):
            first_row(0, cs)
            first_row(1, cs)
            second_row(0, cs)
            send_row(0, columns_half(part))
        if part == 0:
            with jax.named_scope("omega_a"):
                for d in range(1, groups):
                    omega_gather(d)
            lax.fori_loop(EARLY + 1, min(OUTER + 1, chunks), outward, 0)

    def body(i, carry):
        halo_wait(i)
        with jax.named_scope("row"):
            first_row(i + 1)
            step(i)

        @pl.when(i + OUTER < chunks)
        def _():
            halo_start(i + OUTER, False)

        @pl.when(i + INNER < chunks)
        def _():
            halo_start(i + INNER, True)

        return carry

    def omega_finish():
        for d in range(1, groups):
            omega_pair(d).wait_recv()
        for g in range(groups):
            high, low = split(omega[g])
            for k, part in enumerate((high, low, high)):
                omega_parts[g, k * cols : (k + 1) * cols] = part

    def own_row(p, g, up):
        return g * seg + jnp.where(up, p, seg - 1 - p)

    def back(p, d):
        y = own_row(p, me_g, upward)
        here = sketch.at[y]
        at = y - me_g * seg
        return remote(here, here, back_send.at[d - 1, at], back_recv.at[d - 1, at], device(other_group(d), me_b))

    def back_start(lo, hi):
        for p in order[lo:hi]:
            for d in range(1, groups):
                back(p, d).start()

    def rows_of(ref, rows, offset):
        blocks = [ref[own_row(p, me_g, upward) - offset].reshape(slab * span_z, -1) for p in rows]
        return split(jnp.concatenate(blocks, axis=0) if len(blocks) > 1 else blocks[0])

    def columns_of(rows, d):
        return rows_of(grown, rows, 0) if d == 0 else rows_of(cross.at[d - 1], rows, me_g * seg)

    def sketch_batch(rows, start):
        for p in rows:
            at = own_row(p, me_g, upward) - me_g * seg
            for d in range(1, groups):
                here = cross.at[d - 1, at]
                remote(here, here, row_send.at[0], row_recv.at[d - 1, at], sibling).wait_recv()
        left, right = [], []
        for d in range(groups):
            high, low = columns_of(rows, d)
            left += [high, high, low]
            right.append(omega_parts[lax.rem(me_g - d + groups, groups)])
        value = pass_dot(jnp.concatenate(left, axis=1), jnp.concatenate(right, axis=0), ((1,), (0,)))
        size = slab * span_z
        for k, p in enumerate(rows):
            sketch[own_row(p, me_g, upward)] = value[k * size : (k + 1) * size].reshape(slab, span_z, rank)
        high, low = split(value)
        term = pass_dot(high, jnp.concatenate([high, low], axis=1), ((0,), (0,)))
        if start:
            gram[...] = term
        else:
            gram[...] += term

    def project_batch(rows, start):
        value = rows_of(sketch, rows, 0)
        for d in range(groups):
            g = lax.rem(me_g - d + groups, groups)
            term = parts_dot(value, columns_of(rows, d), ((0,), (0,)))
            if start:
                proj[g] = term
            else:
                proj[g] += term

    cutoff = min(plan[0][0], span_y - 3)
    lax.fori_loop(1, cutoff - 1, body, 0)
    with jax.named_scope("omega_b"):
        for d in range(1, groups):
            g = lax.rem(me_g - d + groups, groups)
            gather_finish(
                omega_half(g, core, omega_owners), omega_half(g, core, omega_owners - 1),
                proj_strips.at[pl.ds(0, chips - 1), 0, pl.ds(0, omega_strip)],
                omega_sem.at[d - 1, 0], omega_owners,
            )
            omega_pair(d).start()
    lax.fori_loop(cutoff - 1, cutoff, body, 0)
    done = 0
    for i in range(cutoff, span_y):
        with jax.named_scope("late_row"):
            if i < chunks:
                halo_wait(i)
            if i + 1 < span_y:
                first_row(i + 1)
            step(i)
            if i + OUTER < chunks:
                halo_start(i + OUTER, False)
            if i + INNER < chunks:
                halo_start(i + INNER, True)
        if i == cutoff:
            with jax.named_scope("omega_c"):
                omega_finish()
        while done < len(plan) and plan[done][0] == i:
            rows = plan[done][1]
            with jax.named_scope("sketch"):
                sketch_batch(rows, done == 0)
            done += 1
            if done == 1:
                back_start(0, FIRST_BACK)

    half = pl.ds(pl.multiple_of(core * half_packed, 8), half_packed)
    far_half = pl.ds(pl.multiple_of((1 - core) * half_packed, 8), half_packed)
    mixed = gram[:, rank:]
    gram[:, 0:rank] += mixed + mixed.T
    for k, (i, j) in enumerate(tiles(rank)):
        packed[k * LANES : (k + 1) * LANES] = gram[i * LANES : (i + 1) * LANES, j * LANES : (j + 1) * LANES]
    gram_pair = remote(packed.at[far_half], gram_rx, gram_sem.at[0, 0], gram_sem.at[0, 1], sibling)
    gram_pair.start()
    proj_half = pl.ds(pl.multiple_of(core * (rank // 2), 8), rank // 2)
    proj_far = pl.ds(pl.multiple_of((1 - core) * (rank // 2), 8), rank // 2)
    proj_pair = remote(proj.at[:, proj_far], proj_rx, proj_sem.at[0, 0], proj_sem.at[0, 1], sibling)

    def scatter(source, at, sink, sem, owners, lo, hi):
        def one(d, carry):
            o = chip_peer(d)

            def send():
                remote(at(source, o), sink.at[chip], sem.at[0], sem.at[1], device(me_g, o * 2 + core)).start()

            guarded(owners, o, send)
            return carry

        lax.fori_loop(lo, hi, one, 0)

    def scatter_sum(source, at, sink, sem, owners, result):
        def receive():
            bytes_wait(sink.at[pl.ds(0, chips - 1)], sem.at[1])
            sink[chip] = at(source, chip)[...]
            total = sink[0]
            for o in range(1, chips):
                total = total + sink[o]
            result(total)

        guarded(owners, chip, receive)

    def scatter_sent(sink, sem, owners):
        if owners == chips:
            bytes_wait(sink.at[pl.ds(0, owners - 1)], sem.at[0])
        else:
            @pl.when(chip < owners)
            def _():
                bytes_wait(sink.at[pl.ds(0, owners - 1)], sem.at[0])

            @pl.when(chip >= owners)
            def _():
                bytes_wait(sink.at[pl.ds(0, owners)], sem.at[0])

    def gram_at(ref, o):
        return ref.at[pl.ds(pl.multiple_of(core * half_packed + o * gram_strip, 8), gram_strip)]

    def proj_at(ref, o):
        return ref.at[:, pl.ds(pl.multiple_of(core * (rank // 2) + o * proj_strip_rows, 8), proj_strip_rows)]

    def full_at(ref, o):
        return ref.at[pl.ds(pl.multiple_of(core * (rank // 2) + o * proj_strip_rows, 8), proj_strip_rows)]

    with jax.named_scope("project"):
        for k, (i, rows) in enumerate(plan[:-1]):
            project_batch(rows, k == 0)
    with jax.named_scope("gram_pair"):
        gram_pair.wait_recv()
    packed[half] += gram_rx[...]
    scatter(packed, gram_at, gram_strips, gram_sem.at[1], gram_owners, 1, chips)
    with jax.named_scope("project"):
        project_batch(plan[-1][1], len(plan) == 1)
    proj_pair.start()
    with jax.named_scope("proj_pair"):
        proj_pair.wait_recv()
    proj[:, proj_half] += proj_rx[...]
    scatter(proj, proj_at, proj_strips, proj_sem.at[1], proj_owners, 1, chips)

    def gram_cross(d):
        return remote(
            gram_y.at[me_g], gram_y.at[me_g],
            gram_sem.at[2 + d, 0], gram_sem.at[2 + d, 1], device(other_group(d), me_b),
        )

    def gram_cross_start(total):
        gram_y[me_g] = total
        for d in range(1, groups):
            gram_cross(d).start()

    with jax.named_scope("gram_scatter"):
        scatter_sum(packed, gram_at, gram_strips, gram_sem.at[1], gram_owners, gram_cross_start)
    back_start(FIRST_BACK, SECOND_BACK)

    def proj_cross(d):
        g = other_group(d)
        return remote(
            proj_strip.at[g], proj_y.at[me_g],
            proj_sem.at[2 + d, 0], proj_sem.at[2 + d, 1], device(g, me_b),
        )

    def proj_cross_start(total):
        proj_strip[...] = total
        proj_y[me_g] = proj_strip[me_g]
        for d in range(1, groups):
            proj_cross(d).start()


    def gram_cross_finish():
        for d in range(1, groups):
            gram_cross(d).wait_recv()
        total = gram_y[0]
        for g in range(1, groups):
            total = total + gram_y[g]
        gram_at(gram_full, chip)[...] = total

    def sent(k, carry):
        @pl.when(me_b < bricks - 1)
        def _():
            halo(k, True).wait_send()

        @pl.when(me_b > 0)
        def _():
            halo(k, False).wait_send()

        return carry

    def early_sent():
        for part in range(2):
            @pl.when(me_b < bricks - 1)
            def _():
                halo(0, True, part).wait_send()

            @pl.when(me_b > 0)
            def _():
                halo(0, False, part).wait_send()

        lax.fori_loop(1, chunks, sent, 0)

        def row_sent(y, carry):
            @pl.when(y // seg != me_g)
            def _():
                row_copy(y, y // seg).wait_send()

            return carry

        lax.fori_loop(0, span_y, row_sent, 0)
        for d in range(1, groups):
            guarded(omega_owners, chip, lambda: spread(d).wait_send())
            omega_pair(d).wait_send()

    scatter_sent(gram_strips, gram_sem.at[1], gram_owners)
    with jax.named_scope("gram_cross"):
        guarded(gram_owners, chip, gram_cross_finish)
    gather_start(gram_full, gram_at, gram_sem.at[2], gram_owners)
    early_sent()
    with jax.named_scope("gram_gather"):
        base = pl.multiple_of(core * half_packed, 8)
        gather_finish(
            gram_full.at[half], gram_full.at[pl.ds(base, gram_strip * (gram_owners - 1))],
            gram_strips.at[pl.ds(0, chips - 1)], gram_sem.at[2], gram_owners,
        )
    gram_pair.wait_send()
    gram_join = remote(gram_full.at[half], gram_full.at[half], gram_sem.at[2 + groups, 0], gram_sem.at[2 + groups, 1], sibling)
    gram_join.start()
    def proj_cross_finish():
        for d in range(1, groups):
            proj_cross(d).wait_recv()
        total = proj_y[0]
        for g in range(1, groups):
            total = total + proj_y[g]
        full_at(proj_full, chip)[...] = total

    proj_join = remote(
        proj_full.at[proj_half], proj_full.at[proj_half],
        proj_sem.at[2 + groups, 0], proj_sem.at[2 + groups, 1], sibling,
    )

    def hook_scatter():
        with jax.named_scope("proj_scatter"):
            scatter_sum(proj, proj_at, proj_strips, proj_sem.at[1], proj_owners, proj_cross_start)
        back_start(SECOND_BACK, seg)

    def hook_cross():
        with jax.named_scope("proj_cross"):
            scatter_sent(proj_strips, proj_sem.at[1], proj_owners)
            guarded(proj_owners, chip, proj_cross_finish)
            gather_start(proj_full, full_at, proj_sem.at[2], proj_owners)

    def hook_gather():
        with jax.named_scope("proj_gather"):
            base = pl.multiple_of(core * (rank // 2), 8)
            gather_finish(
                proj_full.at[proj_half], proj_full.at[pl.ds(base, proj_strip_rows * (proj_owners - 1))],
                proj_strips.at[pl.ds(0, chips - 1), 0], proj_sem.at[2], proj_owners,
            )
            proj_pair.wait_send()
            proj_join.start()

    row = lax.broadcasted_iota(jnp.int32, (rank, rank), 0)
    col = lax.broadcasted_iota(jnp.int32, (rank, rank), 1)
    both[:, rank:] = jnp.where(row == col, 1.0, 0.0)
    both[:, 0:rank] = jnp.zeros((rank, rank), jnp.float32)
    hook_scatter()
    with jax.named_scope("gram_join"):
        gram_join.wait_recv()
    for k, (i, j) in enumerate(tiles(rank)):
        both[i * LANES : (i + 1) * LANES, j * LANES : (j + 1) * LANES] = gram_full[k * LANES : (k + 1) * LANES]

    blocks = rank // BLOCK
    eight = lax.broadcasted_iota(jnp.int32, (8, LANES), 0)
    prev_parts, prev_left, prev_right = None, 0, 0
    for block in range(blocks):
        if block == HOOK_CROSS:
            hook_cross()
        at = block * BLOCK
        scope = jax.named_scope("factor")
        scope.__enter__()
        left = at // LANES * LANES
        right = rank + -(-(at + BLOCK) // LANES) * LANES
        panel = both[at : at + BLOCK, left:right]
        if block > 0:
            off, first_lane, common = at - left, left - prev_left, prev_right - left
            mine = outer_product(prev_parts, first_lane, LANES)
            updated = panel[:, :common] - mine[off : off + BLOCK]
            panel = jnp.concatenate([updated, panel[:, common:]], axis=1) if common < right - left else updated
            if off + BLOCK < LANES:
                both[at + BLOCK : left + LANES, left:prev_right] -= mine[off + BLOCK :]
            if left + LANES < rank:
                beyond = outer_product(prev_parts, first_lane + LANES, rank - left - LANES)
                both[left + LANES : rank, left + LANES : prev_right] -= beyond
        high, wide = BLOCK // 8, (right - left) // LANES
        rows = [
            [panel[8 * q : 8 * q + 8, w * LANES : (w + 1) * LANES] for w in range(wide)] for q in range(high)
        ]
        pivots = [jnp.ones((8, LANES), jnp.float32) for _ in range(high)]
        for base in range(0, BLOCK, GROUP):
            columns = {}
            for u in range(base, base + GROUP):
                w, lane = divmod(at - left + u, LANES)
                for q in range(u // 8, high):
                    columns[u, q] = jnp.broadcast_to(rows[q][w][:, lane : lane + 1], (8, LANES))
            for j in range(base, base + GROUP):
                top, r = divmod(j, 8)
                pivot = columns[j, top][r : r + 1]
                over = 1.0 / pivot
                pivots[top] = jnp.where(eight == r, pivot, pivots[top])
                factor = {q: columns[j, q] * over for q in range(top, high)}
                factor[top] = jnp.where(eight > r, factor[top], 0.0)
                for u in range(j + 1, base + GROUP):
                    entry = columns[j, u // 8][u % 8 : u % 8 + 1]
                    for q in range(u // 8, high):
                        columns[u, q] = columns[u, q] - factor[q] * entry
                for w in range(wide):
                    entry = rows[top][w][r : r + 1]
                    for q in range(top, high):
                        rows[q][w] = rows[q][w] - factor[q] * entry
        scales = [lax.rsqrt(pivot) for pivot in pivots]
        prev = jnp.concatenate(
            [jnp.concatenate([x * scales[q] for x in rows[q]], axis=1) for q in range(high)], axis=0
        )
        prev_parts = six_parts(prev)
        prev_left, prev_right = left, right
        both[at : at + BLOCK, left:right] = prev
        scope.__exit__(None, None, None)

    inverse_out[...] = both[:, rank:]
    high, low = split((both[:, rank:] * float(cells) ** 0.5).T)
    for k, part in enumerate((high, low, high)):
        weights[k * rank : (k + 1) * rank] = part

    def write_rows(ys):
        blocks = [sketch[y].reshape(slab * span_z, rank) for y in ys]
        high, low = split(jnp.concatenate(blocks, axis=0) if len(ys) > 1 else blocks[0])
        value = pass_dot(jnp.concatenate([high, high, low], axis=1), weights[...], ((1,), (0,)))
        size = slab * span_z
        for k, y in enumerate(ys):
            basis[:, y] = value[k * size : (k + 1) * size].reshape(slab, span_z, rank)

    with jax.named_scope("basis_own"):
        write_rows([own_row(p, me_g, upward) for p in order])
    def project_final():
        with jax.named_scope("proj_join"):
            proj_join.wait_recv()
        crossed[...] = proj_full[...]

    with jax.named_scope("rows_back"):
        for d in range(1, groups):
            g = lax.rem(me_g - d + groups, groups)
            first_part = max(len(order) - WRITE, 0)
            parts = [order[:first_part]] * (first_part > 0) + [rows for _, rows in plan if rows[0] in order[first_part:]]
            for k, rows in enumerate(parts):
                if d == groups - 1 and k == len(parts) - 1:
                    hook_gather()
                ys = [own_row(p, g, g >= groups // 2) for p in rows]
                with jax.named_scope("row_wait"):
                    for y in ys:
                        here = sketch.at[y]
                        remote(here, here, back_send.at[0, 0], back_recv.at[d - 1, y - g * seg], sibling).wait_recv()
                write_rows(ys)
    project_final()

    with jax.named_scope("sends"):
        for d in range(1, groups):
            for p in order:
                back(p, d).wait_send()
            guarded(gram_owners, chip, lambda: gram_cross(d).wait_send())
            guarded(proj_owners, chip, lambda: proj_cross(d).wait_send())
        gram_join.wait_send()
        proj_join.wait_send()


def store_kernel(basis, inverse, crossed, basis_out, projected_out, projected, sem):
    copies = []
    for i in range(basis.shape[0]):
        copies.append(pltpu.make_async_copy(basis.at[i], basis_out.at[i], sem.at[1 + i]))
        copies[-1].start()
    projected[...] = parts_dot(split(inverse[...]), split(crossed[...]), ((1,), (0,)))
    copies.append(pltpu.make_async_copy(projected, projected_out, sem.at[0]))
    copies[-1].start()
    for copy in copies:
        copy.wait()


def store(basis, inverse, crossed):
    held = lambda x: pltpu.with_memory_space_constraint(x, pltpu.VMEM)
    return pl.pallas_call(
        store_kernel,
        out_shape=tuple(jax.ShapeDtypeStruct(x.shape, x.dtype) for x in (basis, crossed)),
        in_specs=[pl.BlockSpec(memory_space=pltpu.VMEM)] * 3,
        out_specs=[pl.BlockSpec(memory_space=pltpu.HBM)] * 2,
        scratch_shapes=[
            pltpu.VMEM(crossed.shape, jnp.float32),
            pltpu.SemaphoreType.DMA((1 + basis.shape[0],)),
        ],
    )(held(basis), held(inverse), held(crossed))


def shards(groups, bricks, low_factor, test_matrix):
    slab, span_y, span_z, cols = low_factor.shape
    rank = test_matrix.shape[1]
    cells = bricks * slab * span_y * span_z
    chips = bricks // 2
    seg = span_y // groups
    chunks = span_y - LEAD + 1
    total = packed_rows(rank)
    gram_strip = total // 2 // share(total // 2, chips)
    proj_strip = rank // 2 // share(rank // 2, chips)
    vmem = lambda *shape: pltpu.VMEM(shape, jnp.float32)
    dma = pltpu.SemaphoreType.DMA
    basis, inverse, crossed = pl.pallas_call(
        functools.partial(kernel, (groups, bricks, slab, span_y, span_z, cells)),
        out_shape=(
            pltpu.VMEM((slab, span_y, span_z, rank), jnp.float32),
            pltpu.VMEM((rank, rank), jnp.float32),
            pltpu.VMEM((rank, cols), jnp.float32),
        ),
        in_specs=[pl.BlockSpec(memory_space=pltpu.HBM)] * 2,
        out_specs=[pl.BlockSpec(memory_space=pltpu.VMEM)] * 3,
        scratch_shapes=[
            vmem(groups, cols, rank),
            pltpu.VMEM((groups, 3 * cols, rank), jnp.bfloat16),
            pltpu.VMEM((3 * rank, rank), jnp.bfloat16),
            vmem(slab + 4, span_y + 2, span_z, cols),
            vmem(slab + 2, span_y + 2, span_z, cols),
            vmem(span_y, slab, span_z, cols),
            vmem(groups - 1, seg, slab, span_z, cols),
            vmem(span_y, slab, span_z, rank),
            vmem(rank, 2 * rank),
            vmem(total, LANES),
            vmem(total // 2, LANES),
            vmem(chips, gram_strip, LANES),
            vmem(groups, gram_strip, LANES),
            vmem(total, LANES),
            vmem(groups, rank, cols),
            vmem(groups, rank // 2, cols),
            vmem(chips, groups, proj_strip, cols),
            vmem(groups, proj_strip, cols),
            vmem(groups, proj_strip, cols),
            vmem(rank, cols),
            vmem(rank, 2 * rank),
            dma((2,)),
            dma((2, chunks + 1)),
            dma((2, chunks + 1)),
            dma((span_y,)),
            dma((groups - 1, seg)),
            dma((groups - 1, seg)),
            dma((groups - 1, seg)),
            dma((2, groups - 1)),
            dma((groups - 1, 2, 2)),
            dma((3 + groups, 2)),
            dma((3 + groups, 2)),
        ],
        compiler_params=pltpu.CompilerParams(
            collective_id=0, has_side_effects=True, vmem_limit_bytes=48 * 1024 * 1024
        ),
    )(pltpu.with_memory_space_constraint(low_factor, pltpu.HBM), pltpu.with_memory_space_constraint(test_matrix, pltpu.HBM))
    return store(basis, inverse, crossed)


def solution(mesh):
    return jax.shard_map(
        functools.partial(shards, mesh.shape["grp"], mesh.shape["brick"]),
        mesh=mesh,
        in_specs=(P("brick", None, None, "grp"), P("grp", None)),
        out_specs=(P("brick", None, None, None), P(None, "grp")),
        check_vma=False,
    )
```

```python
import functools

import jax
import jax.numpy as jnp
from jax import lax
from jax.experimental import pallas as pl
from jax.experimental.pallas import tpu as pltpu
from jax.sharding import PartitionSpec as P

DIFF = 0.12
CONV = 0.08
MESH = pl.DeviceIdType.MESH
BLOCK = 32
GROUP = 16
LANES = 128
LEAD = 3
OUTER = 4
EARLY = 3
INNER = 6
FIRST_BACK = 3
SECOND_BACK = 5
HOOK_CROSS = 3
WRITE = 4


def split(value):
    high = value.astype(jnp.bfloat16)
    return high, (value - high.astype(jnp.float32)).astype(jnp.bfloat16)


def pass_dot(left, right, dims):
    return lax.dot_general(left, right, (dims, ((), ())), preferred_element_type=jnp.float32)


def parts_dot(left, right, dims):
    (ldim,), (rdim,) = dims
    joined = jnp.concatenate([left[0], left[0], left[1]], axis=ldim)
    return pass_dot(joined, jnp.concatenate([right[0], right[1], right[0]], axis=rdim), dims)


def six_parts(value):
    high, _ = split(value)
    rest = value - high.astype(jnp.float32)
    mid, low = split(rest)
    left = jnp.concatenate([high, high, high, mid, mid, low], axis=0)
    return left, jnp.concatenate([high, mid, low, high, mid, high], axis=0)


def outer_product(parts, start, size):
    return pass_dot(parts[0][:, start : start + size], parts[1][:, start:], ((0,), (0,)))


def share(rows, chips):
    return max(k for k in range(1, chips + 1) if rows % (8 * k) == 0)


def batches(groups, seg, span_y):
    if groups != 2 or seg < 4 or seg % 2:
        return [(span_y - 1, [p]) for p in range(seg)]
    mid = seg // 2
    pairs = [[mid + t, mid - 1 - t] for t in range(mid)]
    lead = (mid + 1) // 2
    return [(seg + mid + lead - 1, sum(pairs[:lead], [])), (span_y - 1, sum(pairs[lead:], []))]


def packed_rows(rank):
    blocks = rank // LANES
    return LANES * blocks * (blocks + 1) // 2


def tiles(rank):
    blocks = rank // LANES
    return [(i, j) for i in range(blocks) for j in range(i, blocks)]


def kernel(
    dims, x_hbm, omega_hbm, basis, inverse_out, crossed,
    omega, omega_parts, weights, ext, first, grown, cross, sketch, gram, packed, gram_rx, gram_strips,
    gram_y, gram_full, proj, proj_rx, proj_strips, proj_strip, proj_y, proj_full, both,
    local_sem, halo_send, halo_recv, row_send, row_recv, back_send, back_recv,
    spread_sem, omega_sem, gram_sem, proj_sem,
):
    groups, bricks, slab, span_y, span_z, cells = dims
    cols, rank = omega.shape[1:]
    chips = bricks // 2
    seg = span_y // groups
    me_g = lax.axis_index("grp")
    me_b = lax.axis_index("brick")
    chip, core = me_b // 2, lax.rem(me_b, 2)
    upward = me_g >= groups // 2
    chunks = span_y - LEAD + 1
    half_packed = packed_rows(rank) // 2
    gram_owners = share(half_packed, chips)
    gram_strip = half_packed // gram_owners
    proj_owners = share(rank // 2, chips)
    proj_strip_rows = rank // 2 // proj_owners
    omega_owners = share(cols // 2, chips)
    omega_strip = cols // 2 // omega_owners
    plan = batches(groups, seg, span_y)
    order = [p for _, rows in plan for p in rows]

    def device(g, b):
        return {"grp": g, "brick": b}

    def other_group(d):
        return lax.rem(me_g + d, groups)

    def chip_peer(d):
        return lax.rem(chip + d, chips)

    sibling = device(me_g, me_b + 1 - 2 * core)
    barrier = pltpu.get_barrier_semaphore()

    def greet(g, b):
        pl.semaphore_signal(barrier, inc=1, device_id=device(g, b), device_id_type=MESH)

    def remote(source, sink, send, recv, to):
        return pltpu.make_async_remote_copy(
            src_ref=source, dst_ref=sink, send_sem=send, recv_sem=recv,
            device_id=to, device_id_type=MESH,
        )

    def bytes_wait(ref, sem):
        pltpu.make_async_copy(ref, ref, sem).wait()

    outer = jnp.where(core == 0, me_b - 1, me_b + 1)
    has_outer = jnp.logical_and(outer >= 0, outer < bricks)
    with jax.named_scope("greet"):
        for d in range(1, groups):
            greet(other_group(d), me_b)
        lax.fori_loop(1, chips, lambda d, c: (greet(me_g, chip_peer(d) * 2 + core), c)[1], 0)

        @pl.when(has_outer)
        def _():
            greet(me_g, outer)

        greet(me_g, me_b + 1 - 2 * core)

    mine = pltpu.make_async_copy(
        x_hbm, ext.at[pl.ds(2, slab), pl.ds(1, span_y)], local_sem.at[0]
    )
    mine.start()
    test = pltpu.make_async_copy(omega_hbm, omega.at[me_g], local_sem.at[1])
    test.start()
    layer = (span_z, cols)
    for y in (0, span_y + 1):
        ext[:, y] = jnp.zeros((slab + 4,) + layer, jnp.float32)
        first[:, y] = jnp.zeros((slab + 2,) + layer, jnp.float32)

    @pl.when(me_b == 0)
    def _():
        ext[0:2] = jnp.zeros((2, span_y + 2) + layer, jnp.float32)

    @pl.when(me_b == bricks - 1)
    def _():
        ext[slab + 2 :] = jnp.zeros((2, span_y + 2) + layer, jnp.float32)

    with jax.named_scope("barrier"):
        pl.semaphore_wait(barrier, groups - 1 + chips + jnp.where(has_outer, 1, 0))

    def row_at(i, count=1):
        return jnp.where(upward, i, span_y - i - count)

    def columns_half(h):
        return pl.ds(h * (cols // 2), cols // 2)

    def halo(k, up, part=None):
        if part is not None:
            start, rows, columns = row_at(0, LEAD), LEAD, columns_half(part)
            k = part * chunks
        else:
            start, rows, columns = row_at(k + LEAD - 1), 1, pl.ds(0, cols)
        side = 0 if up else 1
        return remote(
            x_hbm.at[pl.ds(slab - 2 if up else 0, 2), pl.ds(start, rows), :, columns],
            ext.at[pl.ds(0 if up else slab + 2, 2), pl.ds(1 + start, rows), :, columns],
            halo_send.at[side, k], halo_recv.at[side, k],
            device(me_g, me_b + 1 if up else me_b - 1),
        )

    def halo_start(k, inner, part=None):
        ways = ((core == 0, True), (core == 1, False))
        for sibling_side, up in ways:
            right = sibling_side if inner else jnp.logical_and(jnp.logical_not(sibling_side), has_outer)

            @pl.when(right)
            def _():
                halo(k, up, part).start()

    def halo_wait(k, part=None):
        @pl.when(me_b > 0)
        def _():
            halo(k, True, part).wait_recv()

        @pl.when(me_b < bricks - 1)
        def _():
            halo(k, False, part).wait_recv()

    for part in range(2):
        halo_start(0, False, part)
        halo_start(0, True, part)
    for k in range(1, min(EARLY + 1, chunks)):
        halo_start(k, False)
    test.wait()

    def omega_at(g, o, c):
        return omega.at[g, pl.ds(pl.multiple_of((c * omega_owners + o) * omega_strip, 8), omega_strip)]

    def spread(d):
        here = omega_at(me_g, chip, core)
        return remote(here, here, spread_sem.at[0, d - 1], spread_sem.at[1, d - 1], device(other_group(d), me_b))

    def guarded(owners, index, action):
        if owners == chips:
            action()
        else:
            pl.when(index < owners)(action)

    def spread_start():
        for d in range(1, groups):
            spread(d).start()

    guarded(omega_owners, chip, spread_start)

    def inward(k, carry):
        halo_start(k, True)
        return carry

    def outward(k, carry):
        halo_start(k, False)
        return carry

    lax.fori_loop(1, min(INNER + 1, chunks), inward, 0)
    mine.wait()

    def operate(mid, low, high, before, after):
        z = lax.broadcasted_iota(jnp.int32, mid.shape, mid.ndim - 2)
        down = jnp.where(z == 0, 0.0, pltpu.roll(mid, 1, mid.ndim - 2))
        up = jnp.where(z == span_z - 1, 0.0, pltpu.roll(mid, span_z - 1, mid.ndim - 2))
        beside = low + high + before + after + down + up
        return mid - DIFF * beside - CONV * (low - high)

    gate_low = jnp.where(me_b == 0, 0.0, 1.0)
    gate_high = jnp.where(me_b == bricks - 1, 0.0, 1.0)

    def first_row(i, cs=slice(None)):
        y = row_at(i)
        for i in range(slab + 2):
            value = operate(
                ext[i + 1, y + 1, :, cs], ext[i, y + 1, :, cs], ext[i + 2, y + 1, :, cs],
                ext[i + 1, y, :, cs], ext[i + 1, y + 2, :, cs],
            )
            if i == 0:
                value = value * gate_low
            if i == slab + 1:
                value = value * gate_high
            first[i, y + 1, :, cs] = value

    def second_row(i, cs=slice(None)):
        y = row_at(i)
        for i in range(slab):
            grown[y, i, :, cs] = operate(
                first[i + 1, y + 1, :, cs], first[i, y + 1, :, cs], first[i + 2, y + 1, :, cs],
                first[i + 1, y, :, cs], first[i + 1, y + 2, :, cs],
            )

    def row_copy(y, owner, columns=pl.ds(0, cols)):
        d = lax.rem(owner - me_g + groups, groups)
        at = y - owner * seg
        return remote(
            grown.at[y, :, :, columns], cross.at[d - 1, at, :, :, columns],
            row_send.at[y], row_recv.at[d - 1, at], device(owner, me_b),
        )

    def send_row(i, columns=pl.ds(0, cols)):
        y = row_at(i)
        owner = y // seg

        @pl.when(owner != me_g)
        def _():
            row_copy(y, owner, columns).start()

    def step(i):
        second_row(i)
        send_row(i)

    def gather_start(buf, at, sem, owners):
        def send():
            def one(d, carry):
                here = at(buf, chip)
                remote(here, here, sem.at[0], sem.at[1], device(me_g, chip_peer(d) * 2 + core)).start()
                return carry

            lax.fori_loop(1, chips, one, 0)

        guarded(owners, chip, send)

    def gather_finish(received, all_but_one, sent, sem, owners):
        if owners == chips:
            bytes_wait(all_but_one, sem.at[1])
            bytes_wait(all_but_one, sem.at[0])
        else:
            @pl.when(chip < owners)
            def _():
                bytes_wait(all_but_one, sem.at[1])
                bytes_wait(sent, sem.at[0])

            @pl.when(chip >= owners)
            def _():
                bytes_wait(received, sem.at[1])

    def omega_half(g, c, strips):
        return omega.at[g, pl.ds(pl.multiple_of(c * (cols // 2), 8), strips * omega_strip)]

    def omega_gather(d):
        g = lax.rem(me_g - d + groups, groups)
        guarded(omega_owners, chip, lambda: spread(d).wait_recv())
        gather_start(omega.at[g], lambda ref, o: ref.at[
            pl.ds(pl.multiple_of((core * omega_owners + o) * omega_strip, 8), omega_strip)
        ], omega_sem.at[d - 1, 0], omega_owners)

    def omega_pair(d):
        g = lax.rem(me_g - d + groups, groups)
        here = omega_half(g, core, omega_owners)
        return remote(here, here, omega_sem.at[d - 1, 1, 0], omega_sem.at[d - 1, 1, 1], sibling)

    for part in range(2):
        with jax.named_scope("halo0"):
            halo_wait(0, part)
        cs = slice(part * (cols // 2), (part + 1) * (cols // 2))
        with jax.named_scope("row0"):
            first_row(0, cs)
            first_row(1, cs)
            second_row(0, cs)
            send_row(0, columns_half(part))
        if part == 0:
            with jax.named_scope("omega_a"):
                for d in range(1, groups):
                    omega_gather(d)
            lax.fori_loop(EARLY + 1, min(OUTER + 1, chunks), outward, 0)

    def body(i, carry):
        halo_wait(i)
        with jax.named_scope("row"):
            first_row(i + 1)
            step(i)

        @pl.when(i + OUTER < chunks)
        def _():
            halo_start(i + OUTER, False)

        @pl.when(i + INNER < chunks)
        def _():
            halo_start(i + INNER, True)

        return carry

    def omega_finish():
        for d in range(1, groups):
            omega_pair(d).wait_recv()
        for g in range(groups):
            high, low = split(omega[g])
            for k, part in enumerate((high, low, high)):
                omega_parts[g, k * cols : (k + 1) * cols] = part

    def own_row(p, g, up):
        return g * seg + jnp.where(up, p, seg - 1 - p)

    def back(p, d):
        y = own_row(p, me_g, upward)
        here = sketch.at[y]
        at = y - me_g * seg
        return remote(here, here, back_send.at[d - 1, at], back_recv.at[d - 1, at], device(other_group(d), me_b))

    def back_start(lo, hi):
        for p in order[lo:hi]:
            for d in range(1, groups):
                back(p, d).start()

    def rows_of(ref, rows, offset):
        blocks = [ref[own_row(p, me_g, upward) - offset].reshape(slab * span_z, -1) for p in rows]
        return split(jnp.concatenate(blocks, axis=0) if len(blocks) > 1 else blocks[0])

    def columns_of(rows, d):
        return rows_of(grown, rows, 0) if d == 0 else rows_of(cross.at[d - 1], rows, me_g * seg)

    def sketch_batch(rows, start):
        for p in rows:
            at = own_row(p, me_g, upward) - me_g * seg
            for d in range(1, groups):
                here = cross.at[d - 1, at]
                remote(here, here, row_send.at[0], row_recv.at[d - 1, at], sibling).wait_recv()
        left, right = [], []
        for d in range(groups):
            high, low = columns_of(rows, d)
            left += [high, high, low]
            right.append(omega_parts[lax.rem(me_g - d + groups, groups)])
        value = pass_dot(jnp.concatenate(left, axis=1), jnp.concatenate(right, axis=0), ((1,), (0,)))
        size = slab * span_z
        for k, p in enumerate(rows):
            sketch[own_row(p, me_g, upward)] = value[k * size : (k + 1) * size].reshape(slab, span_z, rank)
        high, low = split(value)
        term = pass_dot(high, jnp.concatenate([high, low], axis=1), ((0,), (0,)))
        if start:
            gram[...] = term
        else:
            gram[...] += term

    def project_batch(rows, start):
        value = rows_of(sketch, rows, 0)
        for d in range(groups):
            g = lax.rem(me_g - d + groups, groups)
            term = parts_dot(value, columns_of(rows, d), ((0,), (0,)))
            if start:
                proj[g] = term
            else:
                proj[g] += term

    cutoff = min(plan[0][0], span_y - 3)
    lax.fori_loop(1, cutoff - 1, body, 0)
    with jax.named_scope("omega_b"):
        for d in range(1, groups):
            g = lax.rem(me_g - d + groups, groups)
            gather_finish(
                omega_half(g, core, omega_owners), omega_half(g, core, omega_owners - 1),
                proj_strips.at[pl.ds(0, chips - 1), 0, pl.ds(0, omega_strip)],
                omega_sem.at[d - 1, 0], omega_owners,
            )
            omega_pair(d).start()
    lax.fori_loop(cutoff - 1, cutoff, body, 0)
    done = 0
    for i in range(cutoff, span_y):
        with jax.named_scope("late_row"):
            if i < chunks:
                halo_wait(i)
            if i + 1 < span_y:
                first_row(i + 1)
            step(i)
            if i + OUTER < chunks:
                halo_start(i + OUTER, False)
            if i + INNER < chunks:
                halo_start(i + INNER, True)
        if i == cutoff:
            with jax.named_scope("omega_c"):
                omega_finish()
        while done < len(plan) and plan[done][0] == i:
            rows = plan[done][1]
            with jax.named_scope("sketch"):
                sketch_batch(rows, done == 0)
            ready = sum(len(part) for _, part in plan[: done + 1])
            if ready >= min(FIRST_BACK, seg) > ready - len(rows):
                back_start(0, FIRST_BACK)
            done += 1

    half = pl.ds(pl.multiple_of(core * half_packed, 8), half_packed)
    far_half = pl.ds(pl.multiple_of((1 - core) * half_packed, 8), half_packed)
    mixed = gram[:, rank:]
    gram[:, 0:rank] += mixed + mixed.T
    for k, (i, j) in enumerate(tiles(rank)):
        packed[k * LANES : (k + 1) * LANES] = gram[i * LANES : (i + 1) * LANES, j * LANES : (j + 1) * LANES]
    gram_pair = remote(packed.at[far_half], gram_rx, gram_sem.at[0, 0], gram_sem.at[0, 1], sibling)
    gram_pair.start()
    proj_half = pl.ds(pl.multiple_of(core * (rank // 2), 8), rank // 2)
    proj_far = pl.ds(pl.multiple_of((1 - core) * (rank // 2), 8), rank // 2)
    proj_pair = remote(proj.at[:, proj_far], proj_rx, proj_sem.at[0, 0], proj_sem.at[0, 1], sibling)

    def scatter(source, at, sink, sem, owners, lo, hi):
        def one(d, carry):
            o = chip_peer(d)

            def send():
                remote(at(source, o), sink.at[chip], sem.at[0], sem.at[1], device(me_g, o * 2 + core)).start()

            guarded(owners, o, send)
            return carry

        lax.fori_loop(lo, hi, one, 0)

    def scatter_sum(source, at, sink, sem, owners, result):
        def receive():
            bytes_wait(sink.at[pl.ds(0, chips - 1)], sem.at[1])
            sink[chip] = at(source, chip)[...]
            total = sink[0]
            for o in range(1, chips):
                total = total + sink[o]
            result(total)

        guarded(owners, chip, receive)

    def scatter_sent(sink, sem, owners):
        if owners == chips:
            bytes_wait(sink.at[pl.ds(0, owners - 1)], sem.at[0])
        else:
            @pl.when(chip < owners)
            def _():
                bytes_wait(sink.at[pl.ds(0, owners - 1)], sem.at[0])

            @pl.when(chip >= owners)
            def _():
                bytes_wait(sink.at[pl.ds(0, owners)], sem.at[0])

    def gram_at(ref, o):
        return ref.at[pl.ds(pl.multiple_of(core * half_packed + o * gram_strip, 8), gram_strip)]

    def proj_at(ref, o):
        return ref.at[:, pl.ds(pl.multiple_of(core * (rank // 2) + o * proj_strip_rows, 8), proj_strip_rows)]

    def full_at(ref, o):
        return ref.at[pl.ds(pl.multiple_of(core * (rank // 2) + o * proj_strip_rows, 8), proj_strip_rows)]

    with jax.named_scope("project"):
        for k, (i, rows) in enumerate(plan[:-1]):
            project_batch(rows, k == 0)
    with jax.named_scope("gram_pair"):
        gram_pair.wait_recv()
    packed[half] += gram_rx[...]
    scatter(packed, gram_at, gram_strips, gram_sem.at[1], gram_owners, 1, chips)
    with jax.named_scope("project"):
        project_batch(plan[-1][1], len(plan) == 1)
    proj_pair.start()
    with jax.named_scope("proj_pair"):
        proj_pair.wait_recv()
    proj[:, proj_half] += proj_rx[...]
    scatter(proj, proj_at, proj_strips, proj_sem.at[1], proj_owners, 1, chips)

    def gram_cross(d):
        return remote(
            gram_y.at[me_g], gram_y.at[me_g],
            gram_sem.at[2 + d, 0], gram_sem.at[2 + d, 1], device(other_group(d), me_b),
        )

    def gram_cross_start(total):
        gram_y[me_g] = total
        for d in range(1, groups):
            gram_cross(d).start()

    with jax.named_scope("gram_scatter"):
        scatter_sum(packed, gram_at, gram_strips, gram_sem.at[1], gram_owners, gram_cross_start)
    back_start(FIRST_BACK, SECOND_BACK)

    def proj_cross(d):
        g = other_group(d)
        return remote(
            proj_strip.at[g], proj_y.at[me_g],
            proj_sem.at[2 + d, 0], proj_sem.at[2 + d, 1], device(g, me_b),
        )

    def proj_cross_start(total):
        proj_strip[...] = total
        proj_y[me_g] = proj_strip[me_g]
        for d in range(1, groups):
            proj_cross(d).start()


    def gram_cross_finish():
        for d in range(1, groups):
            gram_cross(d).wait_recv()
        total = gram_y[0]
        for g in range(1, groups):
            total = total + gram_y[g]
        gram_at(gram_full, chip)[...] = total

    def sent(k, carry):
        @pl.when(me_b < bricks - 1)
        def _():
            halo(k, True).wait_send()

        @pl.when(me_b > 0)
        def _():
            halo(k, False).wait_send()

        return carry

    def early_sent():
        for part in range(2):
            @pl.when(me_b < bricks - 1)
            def _():
                halo(0, True, part).wait_send()

            @pl.when(me_b > 0)
            def _():
                halo(0, False, part).wait_send()

        lax.fori_loop(1, chunks, sent, 0)

        def row_sent(y, carry):
            @pl.when(y // seg != me_g)
            def _():
                row_copy(y, y // seg).wait_send()

            return carry

        lax.fori_loop(0, span_y, row_sent, 0)
        for d in range(1, groups):
            guarded(omega_owners, chip, lambda: spread(d).wait_send())
            omega_pair(d).wait_send()

    scatter_sent(gram_strips, gram_sem.at[1], gram_owners)
    with jax.named_scope("gram_cross"):
        guarded(gram_owners, chip, gram_cross_finish)
    gather_start(gram_full, gram_at, gram_sem.at[2], gram_owners)
    early_sent()
    with jax.named_scope("gram_gather"):
        base = pl.multiple_of(core * half_packed, 8)
        gather_finish(
            gram_full.at[half], gram_full.at[pl.ds(base, gram_strip * (gram_owners - 1))],
            gram_strips.at[pl.ds(0, chips - 1)], gram_sem.at[2], gram_owners,
        )
    gram_pair.wait_send()
    gram_join = remote(gram_full.at[half], gram_full.at[half], gram_sem.at[2 + groups, 0], gram_sem.at[2 + groups, 1], sibling)
    gram_join.start()
    def proj_cross_finish():
        for d in range(1, groups):
            proj_cross(d).wait_recv()
        total = proj_y[0]
        for g in range(1, groups):
            total = total + proj_y[g]
        full_at(proj_full, chip)[...] = total

    proj_join = remote(
        proj_full.at[proj_half], proj_full.at[proj_half],
        proj_sem.at[2 + groups, 0], proj_sem.at[2 + groups, 1], sibling,
    )

    def hook_scatter():
        with jax.named_scope("proj_scatter"):
            scatter_sum(proj, proj_at, proj_strips, proj_sem.at[1], proj_owners, proj_cross_start)
        back_start(SECOND_BACK, seg)

    def hook_cross():
        with jax.named_scope("proj_cross"):
            scatter_sent(proj_strips, proj_sem.at[1], proj_owners)
            guarded(proj_owners, chip, proj_cross_finish)
            gather_start(proj_full, full_at, proj_sem.at[2], proj_owners)

    def hook_gather():
        with jax.named_scope("proj_gather"):
            base = pl.multiple_of(core * (rank // 2), 8)
            gather_finish(
                proj_full.at[proj_half], proj_full.at[pl.ds(base, proj_strip_rows * (proj_owners - 1))],
                proj_strips.at[pl.ds(0, chips - 1), 0], proj_sem.at[2], proj_owners,
            )
            proj_pair.wait_send()
            proj_join.start()

    row = lax.broadcasted_iota(jnp.int32, (rank, rank), 0)
    col = lax.broadcasted_iota(jnp.int32, (rank, rank), 1)
    both[:, rank:] = jnp.where(row == col, 1.0, 0.0)
    both[:, 0:rank] = jnp.zeros((rank, rank), jnp.float32)
    hook_scatter()
    with jax.named_scope("gram_join"):
        gram_join.wait_recv()
    for k, (i, j) in enumerate(tiles(rank)):
        both[i * LANES : (i + 1) * LANES, j * LANES : (j + 1) * LANES] = gram_full[k * LANES : (k + 1) * LANES]

    blocks = rank // BLOCK
    eight = lax.broadcasted_iota(jnp.int32, (8, LANES), 0)
    prev_parts, prev_left, prev_right = None, 0, 0
    for block in range(blocks):
        if block == HOOK_CROSS:
            hook_cross()
        at = block * BLOCK
        scope = jax.named_scope("factor")
        scope.__enter__()
        left = at // LANES * LANES
        right = rank + -(-(at + BLOCK) // LANES) * LANES
        panel = both[at : at + BLOCK, left:right]
        if block > 0:
            off, first_lane, common = at - left, left - prev_left, prev_right - left
            mine = outer_product(prev_parts, first_lane, LANES)
            updated = panel[:, :common] - mine[off : off + BLOCK]
            panel = jnp.concatenate([updated, panel[:, common:]], axis=1) if common < right - left else updated
            if off + BLOCK < LANES:
                both[at + BLOCK : left + LANES, left:prev_right] -= mine[off + BLOCK :]
            if left + LANES < rank:
                beyond = outer_product(prev_parts, first_lane + LANES, rank - left - LANES)
                both[left + LANES : rank, left + LANES : prev_right] -= beyond
        high, wide = BLOCK // 8, (right - left) // LANES
        rows = [
            [panel[8 * q : 8 * q + 8, w * LANES : (w + 1) * LANES] for w in range(wide)] for q in range(high)
        ]
        pivots = [jnp.ones((8, LANES), jnp.float32) for _ in range(high)]
        for base in range(0, BLOCK, GROUP):
            columns = {}
            for u in range(base, base + GROUP):
                w, lane = divmod(at - left + u, LANES)
                for q in range(u // 8, high):
                    columns[u, q] = jnp.broadcast_to(rows[q][w][:, lane : lane + 1], (8, LANES))
            for j in range(base, base + GROUP):
                top, r = divmod(j, 8)
                pivot = columns[j, top][r : r + 1]
                over = 1.0 / pivot
                pivots[top] = jnp.where(eight == r, pivot, pivots[top])
                factor = {q: columns[j, q] * over for q in range(top, high)}
                factor[top] = jnp.where(eight > r, factor[top], 0.0)
                for u in range(j + 1, base + GROUP):
                    entry = columns[j, u // 8][u % 8 : u % 8 + 1]
                    for q in range(u // 8, high):
                        columns[u, q] = columns[u, q] - factor[q] * entry
                for w in range(wide):
                    entry = rows[top][w][r : r + 1]
                    for q in range(top, high):
                        rows[q][w] = rows[q][w] - factor[q] * entry
        scales = [lax.rsqrt(pivot) for pivot in pivots]
        prev = jnp.concatenate(
            [jnp.concatenate([x * scales[q] for x in rows[q]], axis=1) for q in range(high)], axis=0
        )
        prev_parts = six_parts(prev)
        prev_left, prev_right = left, right
        both[at : at + BLOCK, left:right] = prev
        scope.__exit__(None, None, None)

    inverse_out[...] = both[:, rank:]
    high, low = split((both[:, rank:] * float(cells) ** 0.5).T)
    for k, part in enumerate((high, low, high)):
        weights[k * rank : (k + 1) * rank] = part

    def write_rows(ys):
        blocks = [sketch[y].reshape(slab * span_z, rank) for y in ys]
        high, low = split(jnp.concatenate(blocks, axis=0) if len(ys) > 1 else blocks[0])
        value = pass_dot(jnp.concatenate([high, high, low], axis=1), weights[...], ((1,), (0,)))
        size = slab * span_z
        for k, y in enumerate(ys):
            basis[:, y] = value[k * size : (k + 1) * size].reshape(slab, span_z, rank)

    with jax.named_scope("basis_own"):
        write_rows([own_row(p, me_g, upward) for p in order])
    def project_final():
        with jax.named_scope("proj_join"):
            proj_join.wait_recv()
        crossed[...] = proj_full[...]

    with jax.named_scope("rows_back"):
        for d in range(1, groups):
            g = lax.rem(me_g - d + groups, groups)
            first_part = max(len(order) - WRITE, 0)
            parts = [order[:first_part]] * (first_part > 0) + [rows for _, rows in plan if rows[0] in order[first_part:]]
            for k, rows in enumerate(parts):
                if d == groups - 1 and k == len(parts) - 1:
                    hook_gather()
                ys = [own_row(p, g, g >= groups // 2) for p in rows]
                with jax.named_scope("row_wait"):
                    for y in ys:
                        here = sketch.at[y]
                        remote(here, here, back_send.at[0, 0], back_recv.at[d - 1, y - g * seg], sibling).wait_recv()
                write_rows(ys)
    project_final()

    with jax.named_scope("sends"):
        for d in range(1, groups):
            for p in order:
                back(p, d).wait_send()
            guarded(gram_owners, chip, lambda: gram_cross(d).wait_send())
            guarded(proj_owners, chip, lambda: proj_cross(d).wait_send())
        gram_join.wait_send()
        proj_join.wait_send()


def store_kernel(basis, inverse, crossed, basis_out, projected_out, projected, sem):
    copies = []
    for i in range(basis.shape[0]):
        copies.append(pltpu.make_async_copy(basis.at[i], basis_out.at[i], sem.at[1 + i]))
        copies[-1].start()
    projected[...] = parts_dot(split(inverse[...]), split(crossed[...]), ((1,), (0,)))
    copies.append(pltpu.make_async_copy(projected, projected_out, sem.at[0]))
    copies[-1].start()
    for copy in copies:
        copy.wait()


def store(basis, inverse, crossed):
    held = lambda x: pltpu.with_memory_space_constraint(x, pltpu.VMEM)
    return pl.pallas_call(
        store_kernel,
        out_shape=tuple(jax.ShapeDtypeStruct(x.shape, x.dtype) for x in (basis, crossed)),
        in_specs=[pl.BlockSpec(memory_space=pltpu.VMEM)] * 3,
        out_specs=[pl.BlockSpec(memory_space=pltpu.HBM)] * 2,
        scratch_shapes=[
            pltpu.VMEM(crossed.shape, jnp.float32),
            pltpu.SemaphoreType.DMA((1 + basis.shape[0],)),
        ],
    )(held(basis), held(inverse), held(crossed))


def shards(groups, bricks, low_factor, test_matrix):
    slab, span_y, span_z, cols = low_factor.shape
    rank = test_matrix.shape[1]
    cells = bricks * slab * span_y * span_z
    chips = bricks // 2
    seg = span_y // groups
    chunks = span_y - LEAD + 1
    total = packed_rows(rank)
    gram_strip = total // 2 // share(total // 2, chips)
    proj_strip = rank // 2 // share(rank // 2, chips)
    vmem = lambda *shape: pltpu.VMEM(shape, jnp.float32)
    dma = pltpu.SemaphoreType.DMA
    basis, inverse, crossed = pl.pallas_call(
        functools.partial(kernel, (groups, bricks, slab, span_y, span_z, cells)),
        out_shape=(
            pltpu.VMEM((slab, span_y, span_z, rank), jnp.float32),
            pltpu.VMEM((rank, rank), jnp.float32),
            pltpu.VMEM((rank, cols), jnp.float32),
        ),
        in_specs=[pl.BlockSpec(memory_space=pltpu.HBM)] * 2,
        out_specs=[pl.BlockSpec(memory_space=pltpu.VMEM)] * 3,
        scratch_shapes=[
            vmem(groups, cols, rank),
            pltpu.VMEM((groups, 3 * cols, rank), jnp.bfloat16),
            pltpu.VMEM((3 * rank, rank), jnp.bfloat16),
            vmem(slab + 4, span_y + 2, span_z, cols),
            vmem(slab + 2, span_y + 2, span_z, cols),
            vmem(span_y, slab, span_z, cols),
            vmem(groups - 1, seg, slab, span_z, cols),
            vmem(span_y, slab, span_z, rank),
            vmem(rank, 2 * rank),
            vmem(total, LANES),
            vmem(total // 2, LANES),
            vmem(chips, gram_strip, LANES),
            vmem(groups, gram_strip, LANES),
            vmem(total, LANES),
            vmem(groups, rank, cols),
            vmem(groups, rank // 2, cols),
            vmem(chips, groups, proj_strip, cols),
            vmem(groups, proj_strip, cols),
            vmem(groups, proj_strip, cols),
            vmem(rank, cols),
            vmem(rank, 2 * rank),
            dma((2,)),
            dma((2, chunks + 1)),
            dma((2, chunks + 1)),
            dma((span_y,)),
            dma((groups - 1, seg)),
            dma((groups - 1, seg)),
            dma((groups - 1, seg)),
            dma((2, groups - 1)),
            dma((groups - 1, 2, 2)),
            dma((3 + groups, 2)),
            dma((3 + groups, 2)),
        ],
        compiler_params=pltpu.CompilerParams(
            collective_id=0, has_side_effects=True, vmem_limit_bytes=48 * 1024 * 1024
        ),
    )(pltpu.with_memory_space_constraint(low_factor, pltpu.HBM), pltpu.with_memory_space_constraint(test_matrix, pltpu.HBM))
    return store(basis, inverse, crossed)


def solution(mesh):
    return jax.shard_map(
        functools.partial(shards, mesh.shape["grp"], mesh.shape["brick"]),
        mesh=mesh,
        in_specs=(P("brick", None, None, "grp"), P("grp", None)),
        out_specs=(P("brick", None, None, None), P(None, "grp")),
        check_vma=False,
    )
```
